32 devices in a mesh: dp: 4 (over y, core), seq: 8 (over z, x).
Axes of the slice: x: 2, y: 2, z: 4, core: 2. Of those that a mesh axis runs over, the one named last changes fastest.
Arguments:
- inputs: bfloat16 [4, 1024, 2048], P('dp', 'seq'), may hold values from -6 to 6
- w_query: bfloat16 [2048, 2048], P(None, 'seq'), may hold values from -0.125 to 0.125
- sharpness: float32 [32], P('seq'), may hold values from 0.03 to 0.3
- pattern: int32 [8, 2], replicated, may hold values from 0 to 7, as said below
- lengths: int32 [4], P('dp'), may hold values from 512 to 1024
- probes: bfloat16 [4, 1024, 2048], P('dp', 'seq'), may hold values from -36 to 36
- start_vector: float32 [2048], replicated, may hold values from -6 to 6
Outputs:
- branch: bfloat16 [4, 1024, 2048], P('dp', 'seq')
- probe_vjp: bfloat16 [4, 1024, 2048], P('dp', 'seq')
- logdet_terms: float32 [4, 2], P('dp')
- sharpness_grad: float32 [32], P('seq')
- spec_vector: float32 [2048], replicated
- spec_norm: float32 [1], replicated
The draws below stay inside these ranges and needn't reach their ends.
Inputs may be any that keep to these rules, and one draw needn't show every extreme that they name: `pattern`: entry 0 of row I is I itself; the 2 entries of a row differ.
All inputs are finite; a program needn't handle non-finite values.
Results may differ from the reference program's by a relative error of at most 0.007.
Values may be sent and summed in bfloat16 or wider, within the bound.
A program may use at most 64 MiB of HBM per device.

```python
import math
import jax
import jax.numpy as jnp
from jax import lax

D = 2048
HEADS = 32
BLOCK = 128
NB = 2
SEQ_LEN = 1024
SEQS = 4
INNER = 2048


def draw_pattern(key, part):
    block_count = SEQ_LEN // BLOCK
    scores = jax.random.randint(key, (block_count, block_count - 1), 0, 1 << 20) * (block_count - 1)
    scores = scores + jnp.arange(block_count - 1, dtype=jnp.int32)[None, :]
    order = jnp.argsort(scores, axis=1, stable=True)
    offsets = order[:, :NB - 1] + 1
    own_block = jnp.arange(block_count, dtype=jnp.int32)[:, None]
    others = (own_block + offsets) % block_count
    return jnp.concatenate([own_block, others.astype(jnp.int32)], axis=1).astype(jnp.int32)


def draw_lengths(key, part):
    key_a = jax.random.fold_in(key, 11)
    key_b = jax.random.fold_in(key, 12)
    half_len = SEQ_LEN // 2
    drawn = jax.random.randint(key_a, (SEQS,), half_len, SEQ_LEN + 1)
    order = jax.random.permutation(key_b, SEQS)
    drawn = drawn.at[order[0]].set(SEQ_LEN)
    drawn = drawn.at[order[1]].set(half_len)
    return drawn.astype(jnp.int32)


def draw_probes(key, part):
    key_a = jax.random.fold_in(key, 21)
    seq_rise = 1.0 + 2.0 * jnp.arange(SEQS, dtype=jnp.float32) / (SEQS - 1)
    pos_rise = 1.0 + 2.0 * jnp.arange(SEQ_LEN, dtype=jnp.float32) / (SEQ_LEN - 1)
    base = jnp.clip(jax.random.normal(key_a, (SEQS, SEQ_LEN, D), jnp.float32), -4.0, 4.0)
    result = base * seq_rise[:, None, None] * pos_rise[None, :, None]
    return result.astype(jnp.bfloat16)


def levels(rng, dims, shards, least, largest):
    loudness, own = 1.0, jax.random.fold_in(rng, 6)
    for axis_at, shards_of in shards:
        draws = jnp.exp(jax.random.uniform(jax.random.fold_in(own, axis_at), (shards_of,), jnp.float32, least / len(shards), largest / len(shards)))
        loudness = loudness * jnp.repeat(draws, dims[axis_at] // shards_of).reshape([-1 if axis == axis_at else 1 for axis in range(len(dims))])
    return loudness


def normal_values(own_key, extent, width, limit, cuts=(), kind=jnp.bfloat16):
    gain = levels(own_key, extent, cuts, -0.22, 0.18) if cuts else 1.0
    values = jax.random.normal(own_key, extent, jnp.float32) * width * gain
    return jnp.minimum(jnp.maximum(values, -limit), limit).astype(kind)


def setup_inputs(seed: int = 0) -> dict:
    key_list = jax.random.split(jax.random.key(seed), 8)
    inputs = normal_values(key_list[0], (SEQS, SEQ_LEN, D), 1.0, 6.0, ((0, 4), (1, 8)))
    w_query = normal_values(key_list[1], (D, INNER), D ** -0.5, 0.125, ((1, 8),))
    sharpness = jnp.clip(jnp.exp(math.log(0.3) - 2.3025852 * jax.random.uniform(key_list[2], (HEADS,), jnp.float32) ** levels(key_list[2], (HEADS,), ((0, 8),), -0.2, 0.2)), 0.03, 0.3)
    pattern = draw_pattern(jax.random.fold_in(key_list[7], 71), 0)
    lengths = draw_lengths(jax.random.fold_in(key_list[7], 71), 0)
    probes = draw_probes(jax.random.fold_in(key_list[7], 71), 0)
    start_vector = normal_values(key_list[6], (D,), 1.0, 6.0, (), jnp.float32)
    return dict(inputs=inputs, w_query=w_query, sharpness=sharpness, pattern=pattern, lengths=lengths, probes=probes, start_vector=start_vector)


def head_forward(query_head, sharp_head, pattern, length):
    head_size, seq_total = query_head.shape
    block_count, fanout = pattern.shape
    block_len = seq_total // block_count
    query_tiles = jnp.transpose(query_head.reshape(head_size, block_count, block_len), (1, 0, 2))
    key_tiles = jnp.take(query_tiles, pattern, axis=0)
    query_norms = lax.optimization_barrier(jnp.sum(jnp.square(query_tiles.astype(jnp.float32)), axis=1))
    key_norms = jnp.take(query_norms, pattern, axis=0)
    inner_dots = jnp.einsum('qdi,qndj->qinj', query_tiles.astype(jnp.float32), key_tiles.astype(jnp.float32))
    distance = query_norms[:, :, None, None] + key_norms[:, None, :, :] - 2.0 * inner_dots
    query_pos = jnp.arange(block_count, dtype=jnp.int32)[:, None] * block_len + jnp.arange(block_len, dtype=jnp.int32)[None, :]
    key_pos = pattern[:, :, None] * block_len + jnp.arange(block_len, dtype=jnp.int32)[None, None, :]
    allowed = (key_pos[:, None, :, :] < length) | (key_pos[:, None, :, :] == query_pos[:, :, None, None])
    factor = sharp_head / math.sqrt(head_size)
    weights = jnp.where(allowed, jnp.exp(-factor * distance), 0.0)
    totals = lax.optimization_barrier(jnp.sum(weights, axis=(2, 3)))
    softmax = weights / totals[:, :, None, None]
    softmax_low = softmax.astype(jnp.bfloat16)
    mixed_out = jnp.einsum('qinj,qndj->qdi', softmax_low.astype(jnp.float32), key_tiles.astype(jnp.float32))
    attended = jnp.transpose(mixed_out, (1, 0, 2)).reshape(head_size, seq_total)
    return (attended, softmax, softmax_low, distance)

def head_backward(query_head, cotangent, softmax, softmax_low, sharp_head, pattern):
    head_size, seq_total = query_head.shape
    block_count, fanout = pattern.shape
    block_len = seq_total // block_count
    query_tiles = jnp.transpose(query_head.reshape(head_size, block_count, block_len), (1, 0, 2))
    key_tiles = jnp.take(query_tiles, pattern, axis=0)
    co_tiles = jnp.transpose(cotangent.reshape(head_size, block_count, block_len), (1, 0, 2))
    prob_grad = jnp.einsum('qdi,qndj->qinj', co_tiles.astype(jnp.float32), key_tiles.astype(jnp.float32))
    row_inner = lax.optimization_barrier(jnp.sum(softmax * prob_grad, axis=(2, 3)))
    score_grad = softmax * (prob_grad - row_inner[:, :, None, None])
    factor = sharp_head / math.sqrt(head_size)
    coefficient = (-2.0 * factor * score_grad).astype(jnp.bfloat16)
    coef_wide = coefficient.astype(jnp.float32)
    row_total = lax.optimization_barrier(jnp.sum(coef_wide, axis=(2, 3)))
    col_total = lax.optimization_barrier(jnp.sum(coef_wide, axis=1))
    query_part = query_tiles.astype(jnp.float32) * row_total[:, None, :] - jnp.einsum('qinj,qndj->qdi', coef_wide, key_tiles.astype(jnp.float32))
    key_part = key_tiles.astype(jnp.float32) * col_total[:, :, None, :] - jnp.einsum('qinj,qdi->qndj', coef_wide, query_tiles.astype(jnp.float32))
    key_part = key_part + jnp.einsum('qinj,qdi->qndj', softmax_low.astype(jnp.float32), co_tiles.astype(jnp.float32))
    selector = (pattern[:, :, None] == jnp.arange(block_count, dtype=jnp.int32)[None, None, :]).astype(jnp.float32)
    spread = jnp.einsum('qnk,qndj->kdj', selector, key_part, precision=lax.Precision.HIGHEST)
    total_grad = jnp.transpose(query_part + spread, (1, 0, 2)).reshape(head_size, seq_total)
    return (total_grad, score_grad)

def reference(inputs, w_query, sharpness, pattern, lengths, probes, start_vector):
    head_count = sharpness.shape[0]
    width_inner = w_query.shape[1]
    head_size = width_inner // head_count
    seq_total = inputs.shape[1]

    def one_sequence(items):
        tokens, probe_rows, length = items
        valid = (jnp.arange(seq_total, dtype=jnp.int32) < length)[:, None]
        masked = jnp.where(valid, probe_rows, jnp.zeros_like(probe_rows))
        queries = jnp.dot(tokens, w_query, preferred_element_type=jnp.float32).astype(jnp.bfloat16).T.reshape(head_count, head_size, seq_total)
        first_cot = jnp.dot(masked, w_query, preferred_element_type=jnp.float32).astype(jnp.bfloat16).T.reshape(head_count, head_size, seq_total)

        def first_pass(head_items):
            query_head, cot_head, sharp_head = head_items
            attended, softmax, softmax_low, distance = head_forward(query_head, sharp_head, pattern, length)
            grad_one, score_grad = head_backward(query_head, cot_head, softmax, softmax_low, sharp_head, pattern)
            sharp_part = jnp.sum(score_grad * distance) * (-1.0 / math.sqrt(head_size))
            return (attended.astype(jnp.bfloat16), grad_one, sharp_part)
        attended, grad_one, sharp_parts = lax.map(first_pass, (queries, first_cot, sharpness))
        term_one = jnp.sum(grad_one * first_cot.astype(jnp.float32))
        att_rows = attended.reshape(width_inner, seq_total).T
        branch = jnp.dot(att_rows, w_query.T, preferred_element_type=jnp.float32).astype(jnp.bfloat16)
        back_rows = grad_one.astype(jnp.bfloat16).reshape(width_inner, seq_total).T
        probe_vjp = jnp.dot(back_rows, w_query.T, preferred_element_type=jnp.float32).astype(jnp.bfloat16)
        second_cot = jnp.dot(probe_vjp, w_query, preferred_element_type=jnp.float32).astype(jnp.bfloat16).T.reshape(head_count, head_size, seq_total)

        def second_pass(head_items):
            query_head, cot_head, sharp_head = head_items
            attended_again, softmax, softmax_low, distance = head_forward(query_head, sharp_head, pattern, length)
            grad_two, score_grad = head_backward(query_head, cot_head, softmax, softmax_low, sharp_head, pattern)
            return grad_two
        grad_two = lax.map(second_pass, (queries, second_cot, sharpness))
        term_two = jnp.sum(grad_two * first_cot.astype(jnp.float32))
        term_vec = jnp.stack([term_one, term_two]) / (length.astype(jnp.float32) * width_inner)
        return (branch, probe_vjp, term_vec, sharp_parts)
    branch, probe_vjp, logdet_terms, sharp_parts = lax.map(one_sequence, (inputs, probes, lengths))
    sharp_grad = lax.optimization_barrier(jnp.sum(sharp_parts, axis=0)) * (1.0 / (inputs.shape[0] * seq_total * head_size))
    w_wide = w_query.astype(jnp.float32)
    column = jnp.dot(start_vector, w_wide, precision=lax.Precision.HIGHEST)
    image_vec = jnp.dot(w_wide, column, precision=lax.Precision.HIGHEST)
    column_sq = jnp.sum(jnp.square(column))
    spec_vector = image_vec / jnp.sqrt(jnp.mean(jnp.square(image_vec)) + 1e-06)
    spec_norm = jnp.sqrt(jnp.sum(jnp.square(image_vec)) / (column_sq + 1e-06)).reshape(1)
    return (branch, probe_vjp, logdet_terms, sharp_grad, spec_vector, spec_norm)
```

```python
import functools
import math

import jax
import jax.numpy as jnp
from jax import lax
from jax.experimental import pallas as pl
from jax.experimental.pallas import tpu as pltpu
from jax.sharding import PartitionSpec as P

DH = 64
F32 = jnp.float32
BF16 = jnp.bfloat16


def dot(a, b, ca, cb):
    return lax.dot_general(a, b, (((ca,), (cb,)), ((), ())), preferred_element_type=F32)


def attention_kernel(heads, q_ref, c_ref, sharp_ref, pat_ref, len_ref, back_ref, stat_ref,
                     grad, cols):
    blocks, width, span = q_ref.shape
    length = len_ref[0]

    def prepare(i, carry):
        grad[i] = jnp.zeros((width, span), F32)
        q = q_ref[i].astype(F32)
        c = c_ref[i].astype(F32)
        rows = [jnp.sum((q * q)[h * DH:(h + 1) * DH], axis=0, keepdims=True) for h in range(heads)]
        rows += [jnp.sum((q * c)[h * DH:(h + 1) * DH], axis=0, keepdims=True) for h in range(heads)]
        if 2 * heads < 8:
            rows.append(jnp.zeros((8 - 2 * heads, span), F32))
        cols[i] = jnp.transpose(jnp.concatenate(rows, axis=0))
        return carry

    lax.fori_loop(0, blocks, prepare, 0)
    stat_ref[...] = jnp.zeros_like(stat_ref)
    key_at = lax.broadcasted_iota(jnp.int32, (span, span), 0)
    query_at = lax.broadcasted_iota(jnp.int32, (span, span), 1)
    tail = (lax.broadcasted_iota(jnp.int32, (16, 2 * span), 1) < span).astype(F32).astype(BF16)

    def block(i, carry):
        other = pat_ref[i, 1]
        allowed = jnp.concatenate(
            [(i * span + key_at < length) | (key_at == query_at), other * span + key_at < length],
            axis=0)
        for h in range(heads):
            hs = slice(h * DH, (h + 1) * DH)
            q = q_ref[i, hs, :]
            c = c_ref[i, hs, :]
            keys = jnp.concatenate([q, q_ref[other, hs, :]], axis=1)
            key_cots = jnp.concatenate([c, c_ref[other, hs, :]], axis=1)
            qc = jnp.concatenate([q, c], axis=1)
            both = dot(keys, qc, 0, 0)
            inner = both[:, :span]
            prob_grad = both[:, span:]
            cross = dot(key_cots, q, 0, 0)
            qf = q.astype(F32)
            cf = c.astype(F32)
            norm_row = jnp.sum(qf * qf, axis=0, keepdims=True)
            pair_row = jnp.sum(qf * cf, axis=0, keepdims=True)
            norm_col = jnp.concatenate([cols[i, :, h:h + 1], cols[other, :, h:h + 1]], axis=0)
            pair_col = jnp.concatenate(
                [cols[i, :, heads + h:heads + h + 1], cols[other, :, heads + h:heads + h + 1]], axis=0)
            factor = sharp_ref[h] * (1.0 / math.sqrt(DH))
            distance = norm_row + norm_col - 2.0 * inner
            weights = jnp.where(allowed, jnp.exp(-factor * distance), 0.0)
            total = jnp.sum(weights, axis=0, keepdims=True)
            soft = weights * (1.0 / total)
            low = soft.astype(BF16)
            row_inner = jnp.sum(soft * prob_grad, axis=0, keepdims=True)
            score = soft * (prob_grad - row_inner)
            stat_ref[h:h + 1, :] += jnp.sum(score * distance, axis=0, keepdims=True)
            coef = (-2.0 * factor * score).astype(BF16)
            row_total = jnp.sum(coef.astype(F32), axis=0, keepdims=True)
            gap = pair_row + pair_col - cross - prob_grad
            gap_mean = jnp.sum(soft * gap, axis=0, keepdims=True)
            adj = (-2.0 * factor * (soft * (gap - gap_mean))).astype(BF16)
            mixed = jnp.concatenate([coef, low], axis=1)
            left = dot(keys, mixed, 1, 0)
            back_ref[0, i, hs, :] = left[:, span:].astype(BF16)
            adjoint = dot(jnp.concatenate([keys, key_cots], axis=1),
                          jnp.concatenate([adj, low], axis=0), 1, 0)
            back_ref[2, i, hs, :] = adjoint.astype(BF16)
            lhs = jnp.concatenate([jnp.concatenate([-q, c], axis=1), tail], axis=0)
            right = dot(lhs, mixed, 1, 1)
            key_part = keys.astype(F32) * right[DH:DH + 1, :] + right[:DH]
            grad[i, hs, :] += qf * row_total - left[:, :span] + key_part[:, :span]
            grad[other, hs, :] += key_part[:, span:]
        return carry

    lax.fori_loop(0, blocks, block, 0)

    def finish(i, term):
        back_ref[1, i] = grad[i].astype(BF16)
        return term + jnp.sum(grad[i] * c_ref[i].astype(F32), axis=0, keepdims=True)

    stat_ref[heads:heads + 1, :] = lax.fori_loop(0, blocks, finish, jnp.zeros((1, span), F32))


def attention(q, c, sharpness, pattern, lengths):
    blocks, width, span = q.shape
    heads = sharpness.shape[0]
    smem = pl.BlockSpec(memory_space=pltpu.SMEM)
    vmem = pl.BlockSpec(memory_space=pltpu.VMEM)
    return pl.pallas_call(
        functools.partial(attention_kernel, heads),
        out_shape=(jax.ShapeDtypeStruct((3, blocks, width, span), BF16),
                   jax.ShapeDtypeStruct((heads + 1, span), F32)),
        in_specs=[vmem, vmem, smem, smem, smem],
        out_specs=(vmem, vmem),
        scratch_shapes=[pltpu.VMEM((blocks, width, span), F32),
                        pltpu.VMEM((blocks, span, max(8, 2 * heads)), F32)],
        compiler_params=pltpu.CompilerParams(vmem_limit_bytes=40 * 1024 * 1024),
        name="attention",
    )(q, c, sharpness, pattern, lengths)


def shards(inputs, w_query, sharpness, pattern, lengths, probes, start_vector):
    tokens = inputs[0]
    probe_rows = probes[0]
    length = lengths[0]
    rows_here = tokens.shape[0]
    groups = lax.axis_size("seq")
    position = lax.axis_index("seq") * rows_here + jnp.arange(rows_here, dtype=jnp.int32)
    masked = jnp.where((position < length)[:, None], probe_rows, jnp.zeros_like(probe_rows))
    row_share = w_query.shape[0] // lax.axis_size("dp")
    inner_here = w_query.shape[1]
    inner = inner_here * groups
    own_rows = lax.dynamic_slice_in_dim(w_query, lax.axis_index("dp") * row_share, row_share, 0)
    row_band = lax.all_gather(own_rows, "seq", axis=1, tiled=True)
    w_full = lax.all_gather(row_band, "dp", axis=0, tiled=True)
    w_wide = w_query.astype(F32)
    column = jnp.dot(start_vector, w_wide, precision=lax.Precision.HIGHEST)
    image_part = jnp.dot(w_wide, column, precision=lax.Precision.HIGHEST)
    both = jnp.concatenate([tokens, masked], axis=0)
    contract = (((0,), (1,)), ((), ()))
    cols = lax.dot_general(w_full, both, contract, preferred_element_type=F32).astype(BF16)
    sent = cols.reshape(groups, inner_here, 2 * rows_here)
    got = lax.all_to_all(sent, "seq", split_axis=0, concat_axis=0, tiled=True)
    q = got[:, :, :rows_here]
    c = got[:, :, rows_here:]
    back, stats = attention(q, c, sharpness, pattern, lengths)
    home = lax.all_to_all(back, "seq", split_axis=1, concat_axis=1, tiled=True)
    home = home.reshape(3, inner, rows_here)
    branch = lax.dot_general(home[0], w_full, contract, preferred_element_type=F32).astype(BF16)
    probe_vjp = lax.dot_general(home[1], w_full, contract, preferred_element_type=F32).astype(BF16)
    second = lax.dot_general(w_full, probe_vjp, contract, preferred_element_type=F32).astype(BF16)
    heads = sharpness.shape[0]
    term_two = jnp.sum(second.astype(F32) * home[2].astype(F32))
    term_one = jnp.sum(stats[heads])
    seq_total = groups * rows_here
    term_vec = jnp.stack([term_one, term_two]) / (length.astype(F32) * inner)
    scale_down = 1.0 / (lax.axis_size("dp") * seq_total * DH)
    sharp_parts = jnp.sum(stats[:heads], axis=1) * (-1.0 / math.sqrt(DH))
    sharp_grad = lax.psum(sharp_parts, "dp") * scale_down
    term_total, image_vec, column_sq = lax.psum(
        (term_vec, image_part, jnp.sum(jnp.square(column))), "seq")
    spec_vector = image_vec / jnp.sqrt(jnp.mean(jnp.square(image_vec)) + 1e-06)
    spec_norm = jnp.sqrt(jnp.sum(jnp.square(image_vec)) / (column_sq + 1e-06)).reshape(1)
    return (branch[None], probe_vjp[None], term_total.reshape(1, 2), sharp_grad, spec_vector, spec_norm)


def solution(mesh):
    placed = (
        P("dp", "seq", None),
        P(None, "seq"),
        P("seq"),
        P(),
        P("dp"),
        P("dp", "seq", None),
        P(),
    )
    return jax.shard_map(
        shards,
        mesh=mesh,
        in_specs=placed,
        out_specs=(P("dp", "seq", None), P("dp", "seq", None), P("dp", None), P("seq"), P(), P()),
        check_vma=False,
    )
```

```python
import functools
import math

import jax
import jax.numpy as jnp
from jax import lax
from jax.experimental import pallas as pl
from jax.experimental.pallas import tpu as pltpu
from jax.sharding import PartitionSpec as P

DH = 64
F32 = jnp.float32
BF16 = jnp.bfloat16


def dot(a, b, ca, cb):
    return lax.dot_general(a, b, (((ca,), (cb,)), ((), ())), preferred_element_type=F32)


def attention_kernel(heads, q_ref, c_ref, sharp_ref, pat_ref, len_ref, back_ref, stat_ref,
                     grad, cols):
    blocks, width, span = q_ref.shape
    length = len_ref[0]

    def prepare(i, carry):
        grad[i] = jnp.zeros((width, span), F32)
        q = q_ref[i].astype(F32)
        c = c_ref[i].astype(F32)
        rows = [jnp.sum((q * q)[h * DH:(h + 1) * DH], axis=0, keepdims=True) for h in range(heads)]
        rows += [jnp.sum((q * c)[h * DH:(h + 1) * DH], axis=0, keepdims=True) for h in range(heads)]
        if 2 * heads < 8:
            rows.append(jnp.zeros((8 - 2 * heads, span), F32))
        cols[i] = jnp.transpose(jnp.concatenate(rows, axis=0))
        return carry

    lax.fori_loop(0, blocks, prepare, 0)
    stat_ref[...] = jnp.zeros_like(stat_ref)
    key_at = lax.broadcasted_iota(jnp.int32, (span, span), 0)
    query_at = lax.broadcasted_iota(jnp.int32, (span, span), 1)
    tail = (lax.broadcasted_iota(jnp.int32, (16, 2 * span), 1) < span).astype(F32).astype(BF16)

    def block(i, carry):
        other = pat_ref[i, 1]
        allowed = jnp.concatenate(
            [(i * span + key_at < length) | (key_at == query_at), other * span + key_at < length],
            axis=0)
        for h in range(heads):
            hs = slice(h * DH, (h + 1) * DH)
            q = q_ref[i, hs, :]
            c = c_ref[i, hs, :]
            keys = jnp.concatenate([q, q_ref[other, hs, :]], axis=1)
            key_cots = jnp.concatenate([c, c_ref[other, hs, :]], axis=1)
            qc = jnp.concatenate([q, c], axis=1)
            both = dot(keys, qc, 0, 0)
            inner = both[:, :span]
            prob_grad = both[:, span:]
            cross = dot(key_cots, q, 0, 0)
            qf = q.astype(F32)
            cf = c.astype(F32)
            norm_row = jnp.sum(qf * qf, axis=0, keepdims=True)
            pair_row = jnp.sum(qf * cf, axis=0, keepdims=True)
            norm_col = jnp.concatenate([cols[i, :, h:h + 1], cols[other, :, h:h + 1]], axis=0)
            pair_col = jnp.concatenate(
                [cols[i, :, heads + h:heads + h + 1], cols[other, :, heads + h:heads + h + 1]], axis=0)
            factor = sharp_ref[h] * (1.0 / math.sqrt(DH))
            distance = norm_row + norm_col - 2.0 * inner
            weights = jnp.where(allowed, jnp.exp(-factor * distance), 0.0)
            total = jnp.sum(weights, axis=0, keepdims=True)
            soft = weights * (1.0 / total)
            low = soft.astype(BF16)
            row_inner = jnp.sum(soft * prob_grad, axis=0, keepdims=True)
            score = soft * (prob_grad - row_inner)
            stat_ref[h:h + 1, :] += jnp.sum(score * distance, axis=0, keepdims=True)
            coef = (-2.0 * factor * score).astype(BF16)
            row_total = jnp.sum(coef.astype(F32), axis=0, keepdims=True)
            gap = pair_row + pair_col - cross - prob_grad
            gap_mean = jnp.sum(soft * gap, axis=0, keepdims=True)
            adj = (-2.0 * factor * (soft * (gap - gap_mean))).astype(BF16)
            mixed = jnp.concatenate([coef, low], axis=1)
            left = dot(keys, mixed, 1, 0)
            back_ref[0, i, hs, :] = left[:, span:].astype(BF16)
            adjoint = dot(jnp.concatenate([keys, key_cots], axis=1),
                          jnp.concatenate([adj, low], axis=0), 1, 0)
            back_ref[2, i, hs, :] = adjoint.astype(BF16)
            lhs = jnp.concatenate([jnp.concatenate([-q, c], axis=1), tail], axis=0)
            right = dot(lhs, mixed, 1, 1)
            key_part = keys.astype(F32) * right[DH:DH + 1, :] + right[:DH]
            grad[i, hs, :] += qf * row_total - left[:, :span] + key_part[:, :span]
            grad[other, hs, :] += key_part[:, span:]
        return carry

    lax.fori_loop(0, blocks, block, 0)

    def finish(i, term):
        back_ref[1, i] = grad[i].astype(BF16)
        return term + jnp.sum(grad[i] * c_ref[i].astype(F32), axis=0, keepdims=True)

    stat_ref[heads:heads + 1, :] = lax.fori_loop(0, blocks, finish, jnp.zeros((1, span), F32))


def attention(q, c, sharpness, pattern, lengths):
    blocks, width, span = q.shape
    heads = sharpness.shape[0]
    smem = pl.BlockSpec(memory_space=pltpu.SMEM)
    vmem = pl.BlockSpec(memory_space=pltpu.VMEM)
    return pl.pallas_call(
        functools.partial(attention_kernel, heads),
        out_shape=(jax.ShapeDtypeStruct((3, blocks, width, span), BF16),
                   jax.ShapeDtypeStruct((heads + 1, span), F32)),
        in_specs=[vmem, vmem, smem, smem, smem],
        out_specs=(vmem, vmem),
        scratch_shapes=[pltpu.VMEM((blocks, width, span), F32),
                        pltpu.VMEM((blocks, span, max(8, 2 * heads)), F32)],
        compiler_params=pltpu.CompilerParams(vmem_limit_bytes=40 * 1024 * 1024),
        name="attention",
    )(q, c, sharpness, pattern, lengths)


def gather_kernel(ndp, groups, x_ref, p_ref, w_ref, len_ref, start_ref, w_out, got, image_ref,
                  norm_ref, both, outbox, acc, recv, send, a2a_recv, a2a_send):
    span, depth = x_ref.shape
    width = w_ref.shape[1]
    lines, rows = groups // 2, depth // ndp
    ys = ndp // 2
    me, d = lax.axis_index("seq"), lax.axis_index("dp")
    z, x = me // 2, me % 2
    y, core = d // 2, d % 2

    def seq_id(s):
        return {"seq": s, "dp": d}

    def dp_id(t):
        return {"seq": me, "dp": t}

    barrier = pltpu.get_barrier_semaphore()
    for k in range(1, groups):
        pl.semaphore_signal(barrier, inc=1, device_id=seq_id((me + k) % groups),
                            device_id_type=pl.DeviceIdType.MESH)
    pl.semaphore_signal(barrier, inc=1, device_id=dp_id(d + 1 - 2 * core),
                        device_id_type=pl.DeviceIdType.MESH)
    for k in range(1, ys):
        pl.semaphore_signal(barrier, inc=1, device_id=dp_id(((y + k) % ys) * 2 + core),
                            device_id_type=pl.DeviceIdType.MESH)
    pl.semaphore_wait(barrier, groups + ys - 1)

    def piece(s, owner, kind, target, own=False):
        at = pl.ds(pl.multiple_of(owner * rows, rows), rows)
        src = w_ref.at[at] if own else w_out.at[s, at]
        return pltpu.make_async_remote_copy(
            src_ref=src, dst_ref=w_out.at[s, at], send_sem=send.at[kind, s],
            recv_sem=recv.at[owner, s], device_id=target, device_id_type=pl.DeviceIdType.MESH)

    def landed(s, owner):
        at = pl.ds(pl.multiple_of(owner * rows, rows), rows)
        pltpu.make_async_copy(w_out.at[s, at], w_out.at[s, at], recv.at[owner, s]).wait()

    up, down, across = seq_id((me + 2) % groups), seq_id((me + groups - 2) % groups), seq_id(me + 1 - 2 * x)
    mate = dp_id(d + 1 - 2 * core)

    def order(t):
        p, side = t // 2, t % 2
        m = jnp.minimum(z, lines - 1 - z)
        near = jnp.where(p % 2 == 1, z + (p + 1) // 2, z - p // 2)
        far = jnp.where(2 * z < lines, p, lines - 1 - p)
        zs = jnp.where(p <= 2 * m, near, far)
        xs = (x + side) % 2
        return zs * 2 + xs, zs, xs

    pl.when(z + 1 < lines)(lambda: piece(me, d, 0, up, True).start())
    pl.when(z > 0)(lambda: piece(me, d, 1, down, True).start())
    piece(me, d, 2, across, True).start()
    w_out[me] = w_ref[...]
    both[:span] = x_ref[...]
    valid = me * span + lax.broadcasted_iota(jnp.int32, (span, 1), 0) < len_ref[0]
    both[span:] = jnp.where(valid, p_ref[...].astype(F32), 0.0).astype(BF16)
    acc[...] = jnp.zeros_like(acc)
    norm_ref[...] = jnp.zeros_like(norm_ref)

    def stage_a(t):
        s, zs, xs = order(t)
        landed(s, d)

        @pl.when(xs == x)
        def _():
            pl.when((zs < z) & (z + 1 < lines))(lambda: piece(s, d, 0, up).start())
            pl.when((zs > z) & (z > 0))(lambda: piece(s, d, 1, down).start())
            piece(s, d, 2, across).start()

        for k in range(1, ys):
            piece(s, d, 3 + k, dp_id(((y + k) % ys) * 2 + core)).start()
        piece(s, d, 3, mate).start()

    def stage_b(t):
        s, zs, xs = order(t)
        for k in range(1, ys):
            owner = ((y + k) % ys) * 2 + core
            landed(s, owner)
            piece(s, owner, 2 + ys + k, mate).start()

    def out_copy(s):
        return pltpu.make_async_remote_copy(
            src_ref=outbox.at[s], dst_ref=got.at[me], send_sem=a2a_send.at[s],
            recv_sem=a2a_recv.at[me], device_id=seq_id(s), device_id_type=pl.DeviceIdType.MESH)

    def stage_c(t):
        s, zs, xs = order(t)

        @pl.when(t > 0)
        def _():
            for k in range(ys):
                landed(s, ((y + k) % ys) * 2 + 1 - core)

        w = w_out[s]
        res = jnp.transpose(dot(both[...], w, 1, 0)).astype(BF16)

        @pl.when(t > 0)
        def _():
            outbox[s] = res
            out_copy(s).start()

        @pl.when(t == 0)
        def _():
            got[me] = res

        step = 256
        def col_body(r, total):
            at = pl.ds(pl.multiple_of(r * step, step), step)
            part = w_out[s, at, :].astype(F32) * start_ref[at, :]
            return total + jnp.sum(part, axis=0, keepdims=True)

        column = lax.fori_loop(0, depth // step, col_body, jnp.zeros((1, width), F32))
        norm_ref[...] += column * column

        def image_body(r, carry):
            at = pl.ds(pl.multiple_of(r * step, step), step)
            acc[at, :] += w_out[s, at, :].astype(F32) * column
            return carry

        lax.fori_loop(0, depth // step, image_body, 0)

    lag_b, lag_c = 2, 3

    def tick(t, carry):
        pl.when((t > 0) & (t < groups))(lambda: stage_a(t))
        pl.when((t - lag_b > 0) & (t - lag_b < groups))(lambda: stage_b(t - lag_b))
        pl.when(t - lag_c >= 0)(lambda: stage_c(t - lag_c))
        return carry

    lax.fori_loop(0, groups + lag_c, tick, 0)
    image_ref[...] = jnp.sum(acc[...], axis=1, keepdims=True)

    def drain(t, carry):
        s, zs, xs = order(t)
        pl.when((xs == x) & (zs <= z) & (z + 1 < lines))(lambda: piece(s, d, 0, up).wait_send())
        pl.when((xs == x) & (zs >= z) & (z > 0))(lambda: piece(s, d, 1, down).wait_send())
        pl.when(xs == x)(lambda: piece(s, d, 2, across).wait_send())

        @pl.when(t > 0)
        def _():
            for k in range(1, ys):
                piece(s, d, 3 + k, mate).wait_send()
                piece(s, d, 2 + ys + k, mate).wait_send()
            piece(s, d, 3, mate).wait_send()
            out_copy(s).wait_send()
            pltpu.make_async_copy(got.at[s], got.at[s], a2a_recv.at[s]).wait()

        return carry

    lax.fori_loop(0, groups, drain, 0)


def gather_project(ndp, groups, tokens, probe_rows, w_query, lengths, start_vector):
    span, depth = tokens.shape
    width = w_query.shape[1]
    smem = pl.BlockSpec(memory_space=pltpu.SMEM)
    vmem = pl.BlockSpec(memory_space=pltpu.VMEM)
    return pl.pallas_call(
        functools.partial(gather_kernel, ndp, groups),
        out_shape=(jax.ShapeDtypeStruct((groups, depth, width), BF16),
                   jax.ShapeDtypeStruct((groups, width, 2 * span), BF16),
                   jax.ShapeDtypeStruct((depth, 1), F32),
                   jax.ShapeDtypeStruct((1, width), F32)),
        in_specs=[vmem, vmem, vmem, smem, vmem],
        out_specs=(vmem, vmem, vmem, vmem),
        scratch_shapes=[pltpu.VMEM((2 * span, depth), BF16),
                        pltpu.VMEM((groups, width, 2 * span), BF16),
                        pltpu.VMEM((depth, width), F32),
                        pltpu.SemaphoreType.DMA((ndp, groups)),
                        pltpu.SemaphoreType.DMA((2 + ndp, groups)),
                        pltpu.SemaphoreType.DMA((groups,)),
                        pltpu.SemaphoreType.DMA((groups,))],
        compiler_params=pltpu.CompilerParams(collective_id=0, has_side_effects=True,
                                             vmem_limit_bytes=56 * 1024 * 1024),
        name="gather_project",
    )(tokens, probe_rows, w_query, lengths, start_vector.reshape(depth, 1))


def shards(inputs, w_query, sharpness, pattern, lengths, probes, start_vector):
    tokens = inputs[0]
    probe_rows = probes[0]
    length = lengths[0]
    rows_here = tokens.shape[0]
    groups = lax.axis_size("seq")
    inner_here = w_query.shape[1]
    inner = inner_here * groups
    w_all, got, image, norms = gather_project(
        lax.axis_size("dp"), groups, tokens, probe_rows, w_query, lengths, start_vector)
    q = got[:, :, :rows_here]
    c = got[:, :, rows_here:]
    back, stats = attention(q, c, sharpness, pattern, lengths)
    home = lax.all_to_all(back, "seq", split_axis=1, concat_axis=1, tiled=True)
    def spread(block):
        return lax.dot_general(block, w_all, (((0, 1), (0, 2)), ((), ())),
                               preferred_element_type=F32).astype(BF16)

    branch = spread(home[0])
    probe_vjp = spread(home[1])
    second = lax.dot_general(w_all, probe_vjp, (((1,), (1,)), ((), ())),
                             preferred_element_type=F32).astype(BF16)
    heads = sharpness.shape[0]
    term_two = jnp.sum(second.astype(F32) * home[2].astype(F32))
    term_one = jnp.sum(stats[heads])
    seq_total = groups * rows_here
    term_vec = jnp.stack([term_one, term_two]) / (length.astype(F32) * inner)
    scale_down = 1.0 / (lax.axis_size("dp") * seq_total * DH)
    sharp_parts = jnp.sum(stats[:heads], axis=1) * (-1.0 / math.sqrt(DH))
    sharp_grad = lax.psum(sharp_parts, "dp") * scale_down
    term_total = lax.psum(term_vec, "seq")
    image_vec = image.reshape(-1)
    column_sq = jnp.sum(norms)
    spec_vector = image_vec / jnp.sqrt(jnp.mean(jnp.square(image_vec)) + 1e-06)
    spec_norm = jnp.sqrt(jnp.sum(jnp.square(image_vec)) / (column_sq + 1e-06)).reshape(1)
    return (branch[None], probe_vjp[None], term_total.reshape(1, 2), sharp_grad, spec_vector, spec_norm)


def solution(mesh):
    placed = (
        P("dp", "seq", None),
        P(None, "seq"),
        P("seq"),
        P(),
        P("dp"),
        P("dp", "seq", None),
        P(),
    )
    return jax.shard_map(
        shards,
        mesh=mesh,
        in_specs=placed,
        out_specs=(P("dp", "seq", None), P("dp", "seq", None), P("dp", None), P("seq"), P(), P()),
        check_vma=False,
    )
```

```python
import functools
import math

import jax
import jax.numpy as jnp
from jax import lax
from jax.experimental import pallas as pl
from jax.experimental.pallas import tpu as pltpu
from jax.sharding import PartitionSpec as P

DH = 64
F32 = jnp.float32
BF16 = jnp.bfloat16


def dot(a, b, ca, cb):
    return lax.dot_general(a, b, (((ca,), (cb,)), ((), ())), preferred_element_type=F32)


def attention_kernel(heads, ndp, qc_ref, w_ref, sharp_ref, pat_ref, len_ref, branch_ref, vjp_ref,
                     stat_ref, cols, own, other_part, box_a, box_g, home_a, home_g, left_rows,
                     grad_rows, adjoint_out, w_all, seq_tile, dp_tile, w_sem, a_send, a_recv, g_send,
                     g_recv, s_send, s_recv, d_send, d_recv):
    blocks, width, pair = qc_ref.shape
    span = pair // 2
    depth = w_all.shape[1]
    me, d = lax.axis_index("seq"), lax.axis_index("dp")
    length = len_ref[0]
    mesh_id = pl.DeviceIdType.MESH

    fetch = pltpu.make_async_copy(w_ref, w_all, w_sem)
    fetch.start()
    barrier = pltpu.get_barrier_semaphore()
    for k in range(1, blocks):
        pl.semaphore_signal(barrier, inc=1, device_id={"seq": (me + k) % blocks, "dp": d},
                            device_id_type=mesh_id)
    for k in range(1, ndp):
        pl.semaphore_signal(barrier, inc=1, device_id={"seq": me, "dp": (d + k) % ndp},
                            device_id_type=mesh_id)

    def push(src, dst, send, recv, target, t_dp):
        return pltpu.make_async_remote_copy(
            src_ref=src, dst_ref=dst, send_sem=send, recv_sem=recv,
            device_id={"seq": target, "dp": t_dp}, device_id_type=mesh_id)

    def push_a(i):
        return push(box_a.at[i], home_a.at[me], a_send.at[i], a_recv.at[me], i, d)

    def push_g(i):
        return push(box_g.at[i], home_g.at[me], g_send.at[i], g_recv.at[me], i, d)

    def push_s(i):
        return push(seq_tile.at[me], seq_tile.at[me], s_send.at[i], s_recv.at[me], i, d)

    def push_d(j):
        return push(dp_tile.at[d], dp_tile.at[d], d_send.at[j], d_recv.at[d], me, j)

    def arrived(ref, sem):
        pltpu.make_async_copy(ref, ref, sem).wait()

    def prepare(i, carry):
        q = qc_ref[i, :, :span].astype(F32)
        c = qc_ref[i, :, span:].astype(F32)
        rows = [jnp.sum((q * q)[h * DH:(h + 1) * DH], axis=0, keepdims=True) for h in range(heads)]
        rows += [jnp.sum((q * c)[h * DH:(h + 1) * DH], axis=0, keepdims=True) for h in range(heads)]
        if 2 * heads < 8:
            rows.append(jnp.zeros((8 - 2 * heads, span), F32))
        cols[i] = jnp.transpose(jnp.concatenate(rows, axis=0))
        return carry

    lax.fori_loop(0, blocks, prepare, 0)
    sharp_at = dp_tile.at[d]
    sharp_at[...] = jnp.zeros((8, span), F32)
    key_at = lax.broadcasted_iota(jnp.int32, (span, span), 0)
    query_at = lax.broadcasted_iota(jnp.int32, (span, span), 1)
    tail = (lax.broadcasted_iota(jnp.int32, (16, 2 * span), 1) < span).astype(F32).astype(BF16)
    pl.semaphore_wait(barrier, blocks + ndp - 2)

    def block(k, carry):
        i = (me + blocks // 2 + k) % blocks
        other = pat_ref[i, 1]
        allowed = jnp.concatenate(
            [(i * span + key_at < length) | (key_at == query_at), other * span + key_at < length],
            axis=0)
        for h in range(heads):
            hs = slice(h * DH, (h + 1) * DH)
            qc = qc_ref[i, hs, :]
            qc_other = qc_ref[other, hs, :]
            q = qc[:, :span]
            c = qc[:, span:]
            keys = jnp.concatenate([q, qc_other[:, :span]], axis=1)
            key_cots = jnp.concatenate([c, qc_other[:, span:]], axis=1)
            both = dot(keys, qc, 0, 0)
            inner = both[:, :span]
            prob_grad = both[:, span:]
            cross = dot(key_cots, q, 0, 0)
            qf = q.astype(F32)
            cf = c.astype(F32)
            norm_row = jnp.sum(qf * qf, axis=0, keepdims=True)
            pair_row = jnp.sum(qf * cf, axis=0, keepdims=True)
            norm_col = jnp.concatenate([cols[i, :, h:h + 1], cols[other, :, h:h + 1]], axis=0)
            pair_col = jnp.concatenate(
                [cols[i, :, heads + h:heads + h + 1], cols[other, :, heads + h:heads + h + 1]], axis=0)
            factor = sharp_ref[h] * (1.0 / math.sqrt(DH))
            distance = norm_row + norm_col - 2.0 * inner
            weights = jnp.where(allowed, jnp.exp(-factor * distance), 0.0)
            total = jnp.sum(weights, axis=0, keepdims=True)
            soft = weights * (1.0 / total)
            low = soft.astype(BF16)
            row_inner = jnp.sum(soft * prob_grad, axis=0, keepdims=True)
            score = soft * (prob_grad - row_inner)
            dp_tile[d, h:h + 1, :] += jnp.sum(score * distance, axis=0, keepdims=True)
            coef = (-2.0 * factor * score).astype(BF16)
            row_total = jnp.sum(coef.astype(F32), axis=0, keepdims=True)
            gap = pair_row + pair_col - cross - prob_grad
            gap_mean = jnp.sum(soft * gap, axis=0, keepdims=True)
            adj = (-2.0 * factor * (soft * (gap - gap_mean))).astype(BF16)
            mixed = jnp.concatenate([coef, low], axis=1)
            left = dot(keys, mixed, 1, 0)
            box_a[i, 0, hs, :] = left[:, span:].astype(BF16)
            adjoint = dot(jnp.concatenate([keys, key_cots], axis=1),
                          jnp.concatenate([adj, low], axis=0), 1, 0)
            box_a[i, 1, hs, :] = adjoint.astype(BF16)
            lhs = jnp.concatenate([jnp.concatenate([-q, c], axis=1), tail], axis=0)
            right = dot(lhs, mixed, 1, 1)
            key_part = keys.astype(F32) * right[DH:DH + 1, :] + right[:DH]
            own[i, hs, :] = qf * row_total - left[:, :span] + key_part[:, :span]
            other_part[i, hs, :] = key_part[:, span:]
        pl.when(i != me)(lambda: push_a(i).start())
        return carry

    lax.fori_loop(0, blocks, block, 0)

    def finish(k, term):
        m = (me + blocks // 2 + k) % blocks

        def gather(i, total):
            chosen = jnp.where(pat_ref[i, 1] == m, 1.0, 0.0)
            return total + other_part[i] * chosen

        if blocks <= 8:
            g = own[m]
            for i in range(blocks):
                g = gather(i, g)
        else:
            g = lax.fori_loop(0, blocks, gather, own[m])
        box_g[m] = g.astype(BF16)
        pl.when(m != me)(lambda: push_g(m).start())
        return term + jnp.sum(g * qc_ref[m, :, span:].astype(F32), axis=0, keepdims=True)

    term_one = lax.fori_loop(0, blocks, finish, jnp.zeros((1, span), F32))
    for k in range(1, ndp):
        push_d((d + k) % ndp).start()
    home_a[me] = box_a[me]
    home_g[me] = box_g[me]
    fetch.wait()

    def take_a(k, carry):
        s = (me + k) % blocks
        pl.when(k > 0)(lambda: arrived(home_a.at[s], a_recv.at[s]))
        left_rows[s] = jnp.concatenate(
            [jnp.transpose(home_a[s, 0]), jnp.transpose(home_a[s, 1])], axis=0)
        return carry

    lax.fori_loop(0, blocks, take_a, 0)
    step = 256

    def product(rows_ref, r):
        at = pl.ds(pl.multiple_of(r * step, step), step)
        total = jnp.zeros((rows_ref.shape[1], step), F32)
        for s in range(blocks):
            total = total + dot(rows_ref[s], w_all[s, at, :], 1, 1)
        return at, total

    def outward(r, carry):
        at, total = product(left_rows, r)
        branch_ref[:, at] = total[:span].astype(BF16)
        adjoint_out[:, at] = total[span:]
        return carry

    lax.fori_loop(0, depth // step, outward, 0)

    def take_g(k, carry):
        s = (me + k) % blocks
        pl.when(k > 0)(lambda: arrived(home_g.at[s], g_recv.at[s]))
        grad_rows[s] = jnp.transpose(home_g[s])
        return carry

    lax.fori_loop(0, blocks, take_g, 0)

    def backward(r, term):
        at, total = product(grad_rows, r)
        low = total.astype(BF16)
        vjp_ref[:, at] = low
        part = low.astype(F32) * adjoint_out[:, at]
        for n in range(step // span):
            term = term + jnp.sum(part[:, n * span:(n + 1) * span], axis=0, keepdims=True)
        return term

    term_two = lax.fori_loop(0, depth // step, backward, jnp.zeros((1, span), F32))
    seq_tile[me] = jnp.concatenate([term_one, term_two, jnp.zeros((6, span), F32)], axis=0)
    for k in range(1, blocks):
        push_s((me + k) % blocks).start()
    for k in range(1, ndp):
        j = (d + k) % ndp
        arrived(dp_tile.at[j], d_recv.at[j])
        push_d(j).wait_send()
    for k in range(1, blocks):
        i = (me + k) % blocks
        push_a(i).wait_send()
        push_g(i).wait_send()
        arrived(seq_tile.at[i], s_recv.at[i])
        push_s(i).wait_send()
    stat_ref[:8] = jnp.broadcast_to(
        jnp.sum(jnp.sum(seq_tile[...], axis=0), axis=1, keepdims=True), (8, span))
    stat_ref[8:] = jnp.broadcast_to(
        jnp.sum(jnp.sum(dp_tile[...], axis=0), axis=1, keepdims=True), (8, span))


def attention(ndp, qc, w_all, sharpness, pattern, lengths):
    blocks, width, pair = qc.shape
    span = pair // 2
    depth = w_all.shape[1]
    heads = sharpness.shape[0]
    smem = pl.BlockSpec(memory_space=pltpu.SMEM)
    vmem = pl.BlockSpec(memory_space=pltpu.VMEM)
    sem = pltpu.SemaphoreType.DMA
    return pl.pallas_call(
        functools.partial(attention_kernel, heads, ndp),
        out_shape=(jax.ShapeDtypeStruct((span, depth), BF16),
                   jax.ShapeDtypeStruct((span, depth), BF16),
                   jax.ShapeDtypeStruct((16, span), F32)),
        in_specs=[vmem, pl.BlockSpec(memory_space=pl.ANY), smem, smem, smem],
        out_specs=(vmem, vmem, vmem),
        scratch_shapes=[pltpu.VMEM((blocks, span, max(8, 2 * heads)), F32),
                        pltpu.VMEM((blocks, width, span), F32),
                        pltpu.VMEM((blocks, width, span), F32),
                        pltpu.VMEM((blocks, 2, width, span), BF16),
                        pltpu.VMEM((blocks, width, span), BF16),
                        pltpu.VMEM((blocks, 2, width, span), BF16),
                        pltpu.VMEM((blocks, width, span), BF16),
                        pltpu.VMEM((blocks, 2 * span, width), BF16),
                        pltpu.VMEM((blocks, span, width), BF16),
                        pltpu.VMEM((span, depth), F32),
                        pltpu.VMEM((blocks, depth, width), BF16),
                        pltpu.VMEM((blocks, 8, span), F32),
                        pltpu.VMEM((ndp, 8, span), F32),
                        sem, sem((blocks,)), sem((blocks,)), sem((blocks,)), sem((blocks,)),
                        sem((blocks,)), sem((blocks,)), sem((ndp,)), sem((ndp,))],
        compiler_params=pltpu.CompilerParams(collective_id=1, has_side_effects=True,
                                             vmem_limit_bytes=56 * 1024 * 1024),
        name="attention",
    )(qc, w_all, sharpness, pattern, lengths)


def gather_kernel(ndp, groups, x_ref, p_ref, w_ref, len_ref, start_ref, w_out, got, image_ref,
                  norm_ref, both, outbox, acc, recv, send, a2a_recv, a2a_send):
    span, depth = x_ref.shape
    width = w_ref.shape[1]
    lines, rows = groups // 2, depth // ndp
    ys = ndp // 2
    me, d = lax.axis_index("seq"), lax.axis_index("dp")
    z, x = me // 2, me % 2
    y, core = d // 2, d % 2

    def seq_id(s):
        return {"seq": s, "dp": d}

    def dp_id(t):
        return {"seq": me, "dp": t}

    barrier = pltpu.get_barrier_semaphore()
    for k in range(1, groups):
        pl.semaphore_signal(barrier, inc=1, device_id=seq_id((me + k) % groups),
                            device_id_type=pl.DeviceIdType.MESH)
    pl.semaphore_signal(barrier, inc=1, device_id=dp_id(d + 1 - 2 * core),
                        device_id_type=pl.DeviceIdType.MESH)
    for k in range(1, ys):
        pl.semaphore_signal(barrier, inc=1, device_id=dp_id(((y + k) % ys) * 2 + core),
                            device_id_type=pl.DeviceIdType.MESH)
    pl.semaphore_wait(barrier, groups + ys - 1)

    def piece(s, owner, kind, target, own=False):
        at = pl.ds(pl.multiple_of(owner * rows, rows), rows)
        src = w_ref.at[at] if own else w_out.at[s, at]
        return pltpu.make_async_remote_copy(
            src_ref=src, dst_ref=w_out.at[s, at], send_sem=send.at[kind, s],
            recv_sem=recv.at[owner, s], device_id=target, device_id_type=pl.DeviceIdType.MESH)

    def landed(s, owner):
        at = pl.ds(pl.multiple_of(owner * rows, rows), rows)
        pltpu.make_async_copy(w_out.at[s, at], w_out.at[s, at], recv.at[owner, s]).wait()

    up, down, across = seq_id((me + 2) % groups), seq_id((me + groups - 2) % groups), seq_id(me + 1 - 2 * x)
    mate = dp_id(d + 1 - 2 * core)

    def order(t):
        p, side = t // 2, t % 2
        m = jnp.minimum(z, lines - 1 - z)
        near = jnp.where(p % 2 == 1, z + (p + 1) // 2, z - p // 2)
        far = jnp.where(2 * z < lines, p, lines - 1 - p)
        zs = jnp.where(p <= 2 * m, near, far)
        xs = (x + side) % 2
        return zs * 2 + xs, zs, xs

    pl.when(z + 1 < lines)(lambda: piece(me, d, 0, up, True).start())
    pl.when(z > 0)(lambda: piece(me, d, 1, down, True).start())
    piece(me, d, 2, across, True).start()
    w_out[me] = w_ref[...]
    both[:span] = x_ref[...]
    valid = me * span + lax.broadcasted_iota(jnp.int32, (span, 1), 0) < len_ref[0]
    both[span:] = jnp.where(valid, p_ref[...].astype(F32), 0.0).astype(BF16)
    acc[...] = jnp.zeros_like(acc)
    norm_ref[...] = jnp.zeros_like(norm_ref)

    def stage_a(t):
        s, zs, xs = order(t)
        landed(s, d)

        @pl.when(xs == x)
        def _():
            pl.when((zs < z) & (z + 1 < lines))(lambda: piece(s, d, 0, up).start())
            pl.when((zs > z) & (z > 0))(lambda: piece(s, d, 1, down).start())
            piece(s, d, 2, across).start()

        for k in range(1, ys):
            piece(s, d, 3 + k, dp_id(((y + k) % ys) * 2 + core)).start()
        piece(s, d, 3, mate).start()

    def stage_b(t):
        s, zs, xs = order(t)
        for k in range(1, ys):
            owner = ((y + k) % ys) * 2 + core
            landed(s, owner)
            piece(s, owner, 2 + ys + k, mate).start()

    def out_copy(s):
        return pltpu.make_async_remote_copy(
            src_ref=outbox.at[s], dst_ref=got.at[me], send_sem=a2a_send.at[s],
            recv_sem=a2a_recv.at[me], device_id=seq_id(s), device_id_type=pl.DeviceIdType.MESH)

    def stage_c(t):
        s, zs, xs = order(t)

        @pl.when(t > 0)
        def _():
            for k in range(ys):
                landed(s, ((y + k) % ys) * 2 + 1 - core)

        w = w_out[s]
        res = jnp.transpose(dot(both[...], w, 1, 0)).astype(BF16)

        @pl.when(t > 0)
        def _():
            outbox[s] = res
            out_copy(s).start()

        @pl.when(t == 0)
        def _():
            got[me] = res

        step = 256
        def col_body(r, total):
            at = pl.ds(pl.multiple_of(r * step, step), step)
            part = w_out[s, at, :].astype(F32) * start_ref[at, :]
            return total + jnp.sum(part, axis=0, keepdims=True)

        column = lax.fori_loop(0, depth // step, col_body, jnp.zeros((1, width), F32))
        norm_ref[...] += column * column

        def image_body(r, carry):
            at = pl.ds(pl.multiple_of(r * step, step), step)
            acc[at, :] += w_out[s, at, :].astype(F32) * column
            return carry

        lax.fori_loop(0, depth // step, image_body, 0)

    lag_b, lag_c = 2, 3

    def tick(t, carry):
        pl.when((t > 0) & (t < groups))(lambda: stage_a(t))
        pl.when((t - lag_b > 0) & (t - lag_b < groups))(lambda: stage_b(t - lag_b))
        pl.when(t - lag_c >= 0)(lambda: stage_c(t - lag_c))
        return carry

    lax.fori_loop(0, groups + lag_c, tick, 0)
    image_ref[...] = jnp.sum(acc[...], axis=1, keepdims=True)

    def drain(t, carry):
        s, zs, xs = order(t)
        pl.when((xs == x) & (zs <= z) & (z + 1 < lines))(lambda: piece(s, d, 0, up).wait_send())
        pl.when((xs == x) & (zs >= z) & (z > 0))(lambda: piece(s, d, 1, down).wait_send())
        pl.when(xs == x)(lambda: piece(s, d, 2, across).wait_send())

        @pl.when(t > 0)
        def _():
            for k in range(1, ys):
                piece(s, d, 3 + k, mate).wait_send()
                piece(s, d, 2 + ys + k, mate).wait_send()
            piece(s, d, 3, mate).wait_send()
            out_copy(s).wait_send()
            pltpu.make_async_copy(got.at[s], got.at[s], a2a_recv.at[s]).wait()

        return carry

    lax.fori_loop(0, groups, drain, 0)


def gather_project(ndp, groups, tokens, probe_rows, w_query, lengths, start_vector):
    span, depth = tokens.shape
    width = w_query.shape[1]
    smem = pl.BlockSpec(memory_space=pltpu.SMEM)
    vmem = pl.BlockSpec(memory_space=pltpu.VMEM)
    return pl.pallas_call(
        functools.partial(gather_kernel, ndp, groups),
        out_shape=(jax.ShapeDtypeStruct((groups, depth, width), BF16),
                   jax.ShapeDtypeStruct((groups, width, 2 * span), BF16),
                   jax.ShapeDtypeStruct((depth, 1), F32),
                   jax.ShapeDtypeStruct((1, width), F32)),
        in_specs=[vmem, vmem, vmem, smem, vmem],
        out_specs=(vmem, vmem, vmem, vmem),
        scratch_shapes=[pltpu.VMEM((2 * span, depth), BF16),
                        pltpu.VMEM((groups, width, 2 * span), BF16),
                        pltpu.VMEM((depth, width), F32),
                        pltpu.SemaphoreType.DMA((ndp, groups)),
                        pltpu.SemaphoreType.DMA((2 + ndp, groups)),
                        pltpu.SemaphoreType.DMA((groups,)),
                        pltpu.SemaphoreType.DMA((groups,))],
        compiler_params=pltpu.CompilerParams(collective_id=0, has_side_effects=True,
                                             vmem_limit_bytes=56 * 1024 * 1024),
        name="gather_project",
    )(tokens, probe_rows, w_query, lengths, start_vector.reshape(depth, 1))


def shards(inputs, w_query, sharpness, pattern, lengths, probes, start_vector):
    tokens = inputs[0]
    probe_rows = probes[0]
    length = lengths[0]
    rows_here = tokens.shape[0]
    groups = lax.axis_size("seq")
    inner_here = w_query.shape[1]
    inner = inner_here * groups
    w_all, got, image, norms = gather_project(
        lax.axis_size("dp"), groups, tokens, probe_rows, w_query, lengths, start_vector)
    branch, probe_vjp, stats = attention(
        lax.axis_size("dp"), got, w_all, sharpness, pattern, lengths)
    heads = sharpness.shape[0]
    seq_total = groups * rows_here
    term_total = stats[:2, 0] / (length.astype(F32) * inner)
    scale_down = 1.0 / (lax.axis_size("dp") * seq_total * DH)
    sharp_grad = stats[8:8 + heads, 0] * (-1.0 / math.sqrt(DH)) * scale_down
    image_vec = image.reshape(-1)
    column_sq = jnp.sum(norms)
    spec_vector = image_vec / jnp.sqrt(jnp.mean(jnp.square(image_vec)) + 1e-06)
    spec_norm = jnp.sqrt(jnp.sum(jnp.square(image_vec)) / (column_sq + 1e-06)).reshape(1)
    return (branch[None], probe_vjp[None], term_total.reshape(1, 2), sharp_grad, spec_vector, spec_norm)


def solution(mesh):
    placed = (
        P("dp", "seq", None),
        P(None, "seq"),
        P("seq"),
        P(),
        P("dp"),
        P("dp", "seq", None),
        P(),
    )
    return jax.shard_map(
        shards,
        mesh=mesh,
        in_specs=placed,
        out_specs=(P("dp", "seq", None), P("dp", "seq", None), P("dp", None), P("seq"), P(), P()),
        check_vma=False,
    )
```

```python
import functools
import math

import jax
import jax.numpy as jnp
from jax import lax
from jax.experimental import pallas as pl
from jax.experimental.pallas import tpu as pltpu
from jax.sharding import PartitionSpec as P

DH = 64
F32 = jnp.float32
BF16 = jnp.bfloat16


def dot(a, b, ca, cb):
    return lax.dot_general(a, b, (((ca,), (cb,)), ((), ())), preferred_element_type=F32)


def attention_kernel(heads, ndp, qc_ref, w_ref, sharp_ref, pat_ref, len_ref, start_ref, branch_ref,
                     vjp_ref, stat_ref, spec_ref, image, cols, own, other_part, box_a, box_g, home_a, home_g, left_rows,
                     grad_rows, adjoint_out, w_all, seq_tile, dp_tile, w_sem, a_send, a_recv, g_send,
                     g_recv, s_send, s_recv, d_send, d_recv):
    blocks, width, pair = qc_ref.shape
    span = pair // 2
    depth = w_all.shape[1]
    me, d = lax.axis_index("seq"), lax.axis_index("dp")
    length = len_ref[0]
    mesh_id = pl.DeviceIdType.MESH

    fetch = pltpu.make_async_copy(w_ref, w_all, w_sem)
    fetch.start()
    barrier = pltpu.get_barrier_semaphore()
    for k in range(1, blocks):
        pl.semaphore_signal(barrier, inc=1, device_id={"seq": (me + k) % blocks, "dp": d},
                            device_id_type=mesh_id)
    for k in range(1, ndp):
        pl.semaphore_signal(barrier, inc=1, device_id={"seq": me, "dp": (d + k) % ndp},
                            device_id_type=mesh_id)

    def push(src, dst, send, recv, target, t_dp):
        return pltpu.make_async_remote_copy(
            src_ref=src, dst_ref=dst, send_sem=send, recv_sem=recv,
            device_id={"seq": target, "dp": t_dp}, device_id_type=mesh_id)

    def push_a(i):
        return push(box_a.at[i], home_a.at[me], a_send.at[i], a_recv.at[me], i, d)

    def push_g(i):
        return push(box_g.at[i], home_g.at[me], g_send.at[i], g_recv.at[me], i, d)

    def push_s(i):
        return push(seq_tile.at[me], seq_tile.at[me], s_send.at[i], s_recv.at[me], i, d)

    def push_d(j):
        return push(dp_tile.at[d], dp_tile.at[d], d_send.at[j], d_recv.at[d], me, j)

    def arrived(ref, sem):
        pltpu.make_async_copy(ref, ref, sem).wait()

    def prepare(i, carry):
        q = qc_ref[i, :, :span].astype(F32)
        c = qc_ref[i, :, span:].astype(F32)
        rows = [jnp.sum((q * q)[h * DH:(h + 1) * DH], axis=0, keepdims=True) for h in range(heads)]
        rows += [jnp.sum((q * c)[h * DH:(h + 1) * DH], axis=0, keepdims=True) for h in range(heads)]
        if 2 * heads < 8:
            rows.append(jnp.zeros((8 - 2 * heads, span), F32))
        cols[i] = jnp.transpose(jnp.concatenate(rows, axis=0))
        return carry

    lax.fori_loop(0, blocks, prepare, 0)
    sharp_at = dp_tile.at[d]
    sharp_at[...] = jnp.zeros((8, span), F32)
    key_at = lax.broadcasted_iota(jnp.int32, (span, span), 0)
    query_at = lax.broadcasted_iota(jnp.int32, (span, span), 1)
    tail = (lax.broadcasted_iota(jnp.int32, (16, 2 * span), 1) < span).astype(F32).astype(BF16)
    pl.semaphore_wait(barrier, blocks + ndp - 2)

    def block(k, carry):
        i = (me + blocks // 2 + k) % blocks
        other = pat_ref[i, 1]
        allowed = jnp.concatenate(
            [(i * span + key_at < length) | (key_at == query_at), other * span + key_at < length],
            axis=0)
        for h in range(heads):
            hs = slice(h * DH, (h + 1) * DH)
            qc = qc_ref[i, hs, :]
            qc_other = qc_ref[other, hs, :]
            q = qc[:, :span]
            c = qc[:, span:]
            keys = jnp.concatenate([q, qc_other[:, :span]], axis=1)
            key_cots = jnp.concatenate([c, qc_other[:, span:]], axis=1)
            both = dot(keys, qc, 0, 0)
            inner = both[:, :span]
            prob_grad = both[:, span:]
            cross = dot(key_cots, q, 0, 0)
            qf = q.astype(F32)
            cf = c.astype(F32)
            norm_row = jnp.sum(qf * qf, axis=0, keepdims=True)
            pair_row = jnp.sum(qf * cf, axis=0, keepdims=True)
            norm_col = jnp.concatenate([cols[i, :, h:h + 1], cols[other, :, h:h + 1]], axis=0)
            pair_col = jnp.concatenate(
                [cols[i, :, heads + h:heads + h + 1], cols[other, :, heads + h:heads + h + 1]], axis=0)
            factor = sharp_ref[h] * (1.0 / math.sqrt(DH))
            distance = norm_row + norm_col - 2.0 * inner
            weights = jnp.where(allowed, jnp.exp(-factor * distance), 0.0)
            total = jnp.sum(weights, axis=0, keepdims=True)
            soft = weights * (1.0 / total)
            low = soft.astype(BF16)
            row_inner = jnp.sum(soft * prob_grad, axis=0, keepdims=True)
            score = soft * (prob_grad - row_inner)
            dp_tile[d, h:h + 1, :] += jnp.sum(score * distance, axis=0, keepdims=True)
            coef = (-2.0 * factor * score).astype(BF16)
            row_total = jnp.sum(coef.astype(F32), axis=0, keepdims=True)
            gap = pair_row + pair_col - cross - prob_grad
            gap_mean = jnp.sum(soft * gap, axis=0, keepdims=True)
            adj = (-2.0 * factor * (soft * (gap - gap_mean))).astype(BF16)
            mixed = jnp.concatenate([coef, low], axis=1)
            left = dot(keys, mixed, 1, 0)
            box_a[i, 0, hs, :] = left[:, span:].astype(BF16)
            adjoint = dot(jnp.concatenate([keys, key_cots], axis=1),
                          jnp.concatenate([adj, low], axis=0), 1, 0)
            box_a[i, 1, hs, :] = adjoint.astype(BF16)
            lhs = jnp.concatenate([jnp.concatenate([-q, c], axis=1), tail], axis=0)
            right = dot(lhs, mixed, 1, 1)
            key_part = keys.astype(F32) * right[DH:DH + 1, :] + right[:DH]
            own[i, hs, :] = qf * row_total - left[:, :span] + key_part[:, :span]
            other_part[i, hs, :] = key_part[:, span:]
        pl.when(i != me)(lambda: push_a(i).start())
        return carry

    lax.fori_loop(0, blocks, block, 0)

    def finish(k, term):
        m = (me + blocks // 2 + k) % blocks

        def gather(i, total):
            chosen = jnp.where(pat_ref[i, 1] == m, 1.0, 0.0)
            return total + other_part[i] * chosen

        if blocks <= 8:
            g = own[m]
            for i in range(blocks):
                g = gather(i, g)
        else:
            g = lax.fori_loop(0, blocks, gather, own[m])
        box_g[m] = g.astype(BF16)
        pl.when(m != me)(lambda: push_g(m).start())
        return term + jnp.sum(g * qc_ref[m, :, span:].astype(F32), axis=0, keepdims=True)

    term_one = lax.fori_loop(0, blocks, finish, jnp.zeros((1, span), F32))
    for k in range(1, ndp):
        push_d((d + k) % ndp).start()
    home_a[me] = box_a[me]
    home_g[me] = box_g[me]
    fetch.wait()

    def take_a(k, carry):
        s = (me + k) % blocks
        pl.when(k > 0)(lambda: arrived(home_a.at[s], a_recv.at[s]))
        left_rows[s, :2 * span, :] = jnp.concatenate(
            [jnp.transpose(home_a[s, 0]), jnp.transpose(home_a[s, 1])], axis=0)
        return carry

    def split(v):
        high = v.astype(BF16).astype(F32)
        mid = (v - high).astype(BF16).astype(F32)
        rows = [high, mid, v - high - mid, jnp.zeros((13, v.shape[1]), F32)]
        return jnp.concatenate(rows, axis=0).astype(BF16)

    start_rows = split(start_ref[...])

    def power(s, total):
        column = jnp.sum(dot(start_rows, w_all[s], 1, 0), axis=0, keepdims=True)
        left_rows[s, 2 * span:, :] = split(column)
        return total + column * column

    column_sq = lax.fori_loop(0, blocks, power, jnp.zeros((1, width), F32))
    lax.fori_loop(0, blocks, take_a, 0)
    step = 256

    def product(rows_ref, r):
        at = pl.ds(pl.multiple_of(r * step, step), step)
        total = jnp.zeros((rows_ref.shape[1], step), F32)
        for s in range(blocks):
            total = total + dot(rows_ref[s], w_all[s, at, :], 1, 1)
        return at, total

    def outward(r, carry):
        at, total = product(left_rows, r)
        branch_ref[:, at] = total[:span].astype(BF16)
        adjoint_out[:, at] = total[span:2 * span]
        image[:, at] = jnp.sum(total[2 * span:], axis=0, keepdims=True)
        return carry

    lax.fori_loop(0, depth // step, outward, 0)

    def take_g(k, carry):
        s = (me + k) % blocks
        pl.when(k > 0)(lambda: arrived(home_g.at[s], g_recv.at[s]))
        grad_rows[s] = jnp.transpose(home_g[s])
        return carry

    lax.fori_loop(0, blocks, take_g, 0)

    def backward(r, term):
        at, total = product(grad_rows, r)
        low = total.astype(BF16)
        vjp_ref[:, at] = low
        part = low.astype(F32) * adjoint_out[:, at]
        for n in range(step // span):
            term = term + jnp.sum(part[:, n * span:(n + 1) * span], axis=0, keepdims=True)
        return term

    image_sq = jnp.sum(image[...] * image[...], axis=1, keepdims=True)
    spec_ref[...] = image[...] / jnp.sqrt(image_sq / depth + 1e-06)
    norm = jnp.sqrt(image_sq / (jnp.sum(column_sq, axis=1, keepdims=True) + 1e-06))
    stat_ref[16:] = jnp.broadcast_to(norm, (8, span))
    term_two = lax.fori_loop(0, depth // step, backward, jnp.zeros((1, span), F32))
    seq_tile[me] = jnp.concatenate([term_one, term_two, jnp.zeros((6, span), F32)], axis=0)
    for k in range(1, blocks):
        push_s((me + k) % blocks).start()
    for k in range(1, ndp):
        j = (d + k) % ndp
        arrived(dp_tile.at[j], d_recv.at[j])
        push_d(j).wait_send()
    for k in range(1, blocks):
        i = (me + k) % blocks
        push_a(i).wait_send()
        push_g(i).wait_send()
        arrived(seq_tile.at[i], s_recv.at[i])
        push_s(i).wait_send()
    stat_ref[:8] = jnp.broadcast_to(
        jnp.sum(jnp.sum(seq_tile[...], axis=0), axis=1, keepdims=True), (8, span))
    stat_ref[8:16] = jnp.broadcast_to(
        jnp.sum(jnp.sum(dp_tile[...], axis=0), axis=1, keepdims=True), (8, span))


def attention(ndp, qc, w_all, sharpness, pattern, lengths, start_vector):
    blocks, width, pair = qc.shape
    span = pair // 2
    depth = w_all.shape[1]
    heads = sharpness.shape[0]
    smem = pl.BlockSpec(memory_space=pltpu.SMEM)
    vmem = pl.BlockSpec(memory_space=pltpu.VMEM)
    sem = pltpu.SemaphoreType.DMA
    return pl.pallas_call(
        functools.partial(attention_kernel, heads, ndp),
        out_shape=(jax.ShapeDtypeStruct((span, depth), BF16),
                   jax.ShapeDtypeStruct((span, depth), BF16),
                   jax.ShapeDtypeStruct((24, span), F32),
                   jax.ShapeDtypeStruct((1, depth), F32)),
        in_specs=[vmem, pl.BlockSpec(memory_space=pl.ANY), smem, smem, smem, vmem],
        out_specs=(vmem, vmem, vmem, vmem),
        scratch_shapes=[pltpu.VMEM((1, depth), F32),
                        pltpu.VMEM((blocks, span, max(8, 2 * heads)), F32),
                        pltpu.VMEM((blocks, width, span), F32),
                        pltpu.VMEM((blocks, width, span), F32),
                        pltpu.VMEM((blocks, 2, width, span), BF16),
                        pltpu.VMEM((blocks, width, span), BF16),
                        pltpu.VMEM((blocks, 2, width, span), BF16),
                        pltpu.VMEM((blocks, width, span), BF16),
                        pltpu.VMEM((blocks, 2 * span + 16, width), BF16),
                        pltpu.VMEM((blocks, span, width), BF16),
                        pltpu.VMEM((span, depth), F32),
                        pltpu.VMEM((blocks, depth, width), BF16),
                        pltpu.VMEM((blocks, 8, span), F32),
                        pltpu.VMEM((ndp, 8, span), F32),
                        sem, sem((blocks,)), sem((blocks,)), sem((blocks,)), sem((blocks,)),
                        sem((blocks,)), sem((blocks,)), sem((ndp,)), sem((ndp,))],
        compiler_params=pltpu.CompilerParams(collective_id=1, has_side_effects=True,
                                             vmem_limit_bytes=56 * 1024 * 1024),
        name="attention",
    )(qc, w_all, sharpness, pattern, lengths, start_vector.reshape(1, depth))


def keep_kernel(a_ref, b_ref, a_out, b_out):
    a_out[...] = a_ref[...]
    b_out[...] = b_ref[...]


def keep(a, b):
    vmem = pl.BlockSpec(memory_space=pltpu.VMEM)
    shape = jax.ShapeDtypeStruct(a.shape, a.dtype)
    return pl.pallas_call(keep_kernel, out_shape=(shape, shape), in_specs=[vmem, vmem],
                          out_specs=(vmem, vmem), name="keep")(a, b)


def gather_kernel(ndp, groups, x_ref, p_ref, w_ref, len_ref, w_out, got, both, outbox, recv, send, a2a_recv, a2a_send):
    span, depth = x_ref.shape
    width = w_ref.shape[1]
    lines, rows = groups // 2, depth // ndp
    ys = ndp // 2
    me, d = lax.axis_index("seq"), lax.axis_index("dp")
    z, x = me // 2, me % 2
    y, core = d // 2, d % 2

    def seq_id(s):
        return {"seq": s, "dp": d}

    def dp_id(t):
        return {"seq": me, "dp": t}

    barrier = pltpu.get_barrier_semaphore()
    for k in range(1, groups):
        pl.semaphore_signal(barrier, inc=1, device_id=seq_id((me + k) % groups),
                            device_id_type=pl.DeviceIdType.MESH)
    pl.semaphore_signal(barrier, inc=1, device_id=dp_id(d + 1 - 2 * core),
                        device_id_type=pl.DeviceIdType.MESH)
    for k in range(1, ys):
        pl.semaphore_signal(barrier, inc=1, device_id=dp_id(((y + k) % ys) * 2 + core),
                            device_id_type=pl.DeviceIdType.MESH)
    pl.semaphore_wait(barrier, groups + ys - 1)

    def piece(s, owner, kind, target, own=False):
        at = pl.ds(pl.multiple_of(owner * rows, rows), rows)
        src = w_ref.at[at] if own else w_out.at[s, at]
        return pltpu.make_async_remote_copy(
            src_ref=src, dst_ref=w_out.at[s, at], send_sem=send.at[kind, s],
            recv_sem=recv.at[owner, s], device_id=target, device_id_type=pl.DeviceIdType.MESH)

    def landed(s, owner):
        at = pl.ds(pl.multiple_of(owner * rows, rows), rows)
        pltpu.make_async_copy(w_out.at[s, at], w_out.at[s, at], recv.at[owner, s]).wait()

    up, down, across = seq_id((me + 2) % groups), seq_id((me + groups - 2) % groups), seq_id(me + 1 - 2 * x)
    mate = dp_id(d + 1 - 2 * core)

    def order(t):
        p, side = t // 2, t % 2
        m = jnp.minimum(z, lines - 1 - z)
        near = jnp.where(p % 2 == 1, z + (p + 1) // 2, z - p // 2)
        far = jnp.where(2 * z < lines, p, lines - 1 - p)
        zs = jnp.where(p <= 2 * m, near, far)
        xs = (x + side) % 2
        return zs * 2 + xs, zs, xs

    pl.when(z + 1 < lines)(lambda: piece(me, d, 0, up, True).start())
    pl.when(z > 0)(lambda: piece(me, d, 1, down, True).start())
    piece(me, d, 2, across, True).start()
    for k in range(1, ys):
        piece(me, ((y + k) % ys) * 2 + core, 3 + k, across, True).start()
    w_out[me] = w_ref[...]
    both[:span] = x_ref[...]
    valid = me * span + lax.broadcasted_iota(jnp.int32, (span, 1), 0) < len_ref[0]
    both[span:] = jnp.where(valid, p_ref[...].astype(F32), 0.0).astype(BF16)

    def stage_a(t):
        s, zs, xs = order(t)
        landed(s, d)

        @pl.when(xs == x)
        def _():
            pl.when((zs < z) & (z + 1 < lines))(lambda: piece(s, d, 0, up).start())
            pl.when((zs > z) & (z > 0))(lambda: piece(s, d, 1, down).start())
            piece(s, d, 2, across).start()

        @pl.when(t > 1)
        def _():
            for k in range(1, ys):
                piece(s, d, 3 + k, dp_id(((y + k) % ys) * 2 + core)).start()

        piece(s, d, 3, mate).start()

    def stage_b(t):
        s, zs, xs = order(t)
        for k in range(1, ys):
            owner = ((y + k) % ys) * 2 + core
            landed(s, owner)
            piece(s, owner, 2 + ys + k, mate).start()

    def out_copy(s):
        return pltpu.make_async_remote_copy(
            src_ref=outbox.at[s], dst_ref=got.at[me], send_sem=a2a_send.at[s],
            recv_sem=a2a_recv.at[me], device_id=seq_id(s), device_id_type=pl.DeviceIdType.MESH)

    def stage_c(t):
        s, zs, xs = order(t)

        @pl.when(t > 0)
        def _():
            for k in range(ys):
                landed(s, ((y + k) % ys) * 2 + 1 - core)

        w = w_out[s]
        res = jnp.transpose(dot(both[...], w, 1, 0)).astype(BF16)

        @pl.when(t > 0)
        def _():
            outbox[s] = res
            out_copy(s).start()

        @pl.when(t == 0)
        def _():
            got[me] = res

    lag_b, lag_c = 2, 3

    def tick(t, carry):
        pl.when((t > 0) & (t < groups))(lambda: stage_a(t))
        pl.when((t - lag_b > 0) & (t - lag_b < groups))(lambda: stage_b(t - lag_b))
        pl.when(t - lag_c >= 0)(lambda: stage_c(t - lag_c))
        return carry

    lax.fori_loop(0, groups + lag_c, tick, 0)

    def drain(t, carry):
        s, zs, xs = order(t)
        pl.when((xs == x) & (zs <= z) & (z + 1 < lines))(lambda: piece(s, d, 0, up).wait_send())
        pl.when((xs == x) & (zs >= z) & (z > 0))(lambda: piece(s, d, 1, down).wait_send())
        pl.when(xs == x)(lambda: piece(s, d, 2, across).wait_send())

        @pl.when(t != 1)
        def _():
            for k in range(1, ys):
                piece(s, d, 3 + k, mate).wait_send()

        @pl.when(t > 0)
        def _():
            for k in range(1, ys):
                piece(s, d, 2 + ys + k, mate).wait_send()
            piece(s, d, 3, mate).wait_send()
            out_copy(s).wait_send()
            pltpu.make_async_copy(got.at[s], got.at[s], a2a_recv.at[s]).wait()

        return carry

    lax.fori_loop(0, groups, drain, 0)


def gather_project(ndp, groups, tokens, probe_rows, w_query, lengths):
    span, depth = tokens.shape
    width = w_query.shape[1]
    smem = pl.BlockSpec(memory_space=pltpu.SMEM)
    vmem = pl.BlockSpec(memory_space=pltpu.VMEM)
    return pl.pallas_call(
        functools.partial(gather_kernel, ndp, groups),
        out_shape=(jax.ShapeDtypeStruct((groups, depth, width), BF16),
                   jax.ShapeDtypeStruct((groups, width, 2 * span), BF16)),
        in_specs=[vmem, vmem, vmem, smem],
        out_specs=(vmem, vmem),
        scratch_shapes=[pltpu.VMEM((2 * span, depth), BF16),
                        pltpu.VMEM((groups, width, 2 * span), BF16),
                        pltpu.SemaphoreType.DMA((ndp, groups)),
                        pltpu.SemaphoreType.DMA((2 + ndp, groups)),
                        pltpu.SemaphoreType.DMA((groups,)),
                        pltpu.SemaphoreType.DMA((groups,))],
        compiler_params=pltpu.CompilerParams(collective_id=0, has_side_effects=True,
                                             vmem_limit_bytes=56 * 1024 * 1024),
        name="gather_project",
    )(tokens, probe_rows, w_query, lengths)


def shards(inputs, w_query, sharpness, pattern, lengths, probes, start_vector):
    tokens = inputs[0]
    probe_rows = probes[0]
    length = lengths[0]
    rows_here = tokens.shape[0]
    groups = lax.axis_size("seq")
    inner_here = w_query.shape[1]
    inner = inner_here * groups
    w_all, got = gather_project(
        lax.axis_size("dp"), groups, tokens, probe_rows, w_query, lengths)
    branch, probe_vjp, stats, spec = attention(
        lax.axis_size("dp"), got, w_all, sharpness, pattern, lengths, start_vector)
    branch, probe_vjp = keep(branch, probe_vjp)
    heads = sharpness.shape[0]
    seq_total = groups * rows_here
    term_total = stats[:2, 0] / (length.astype(F32) * inner)
    scale_down = 1.0 / (lax.axis_size("dp") * seq_total * DH)
    sharp_grad = stats[8:8 + heads, 0] * (-1.0 / math.sqrt(DH)) * scale_down
    spec_vector = spec.reshape(-1)
    spec_norm = stats[16, :1]
    return (branch[None], probe_vjp[None], term_total.reshape(1, 2), sharp_grad, spec_vector, spec_norm)


def solution(mesh):
    placed = (
        P("dp", "seq", None),
        P(None, "seq"),
        P("seq"),
        P(),
        P("dp"),
        P("dp", "seq", None),
        P(),
    )
    return jax.shard_map(
        shards,
        mesh=mesh,
        in_specs=placed,
        out_specs=(P("dp", "seq", None), P("dp", "seq", None), P("dp", None), P("seq"), P(), P()),
        check_vma=False,
    )
```

```python
import functools
import math

import jax
import jax.numpy as jnp
from jax import lax
from jax.experimental import pallas as pl
from jax.experimental.pallas import tpu as pltpu
from jax.sharding import PartitionSpec as P

DH = 64
F32 = jnp.float32
BF16 = jnp.bfloat16


def dot(a, b, ca, cb):
    return lax.dot_general(a, b, (((ca,), (cb,)), ((), ())), preferred_element_type=F32)


def attention_kernel(heads, ndp, qc_ref, w_ref, sharp_ref, pat_ref, len_ref, start_ref, branch_ref,
                     vjp_ref, stat_ref, spec_ref, image, cols, own, other_part, box_a, box_g, home_a, home_g, left_rows,
                     grad_rows, adjoint_out, w_all, seq_tile, dp_tile, w_sem, a_send, a_recv, g_send,
                     g_recv, s_send, s_recv, d_send, d_recv):
    blocks, width, pair = qc_ref.shape
    span = pair // 2
    depth = w_all.shape[1]
    me, d = lax.axis_index("seq"), lax.axis_index("dp")
    length = len_ref[0]
    mesh_id = pl.DeviceIdType.MESH

    fetch = pltpu.make_async_copy(w_ref, w_all, w_sem)
    fetch.start()
    barrier = pltpu.get_barrier_semaphore()
    for k in range(1, blocks):
        pl.semaphore_signal(barrier, inc=1, device_id={"seq": (me + k) % blocks, "dp": d},
                            device_id_type=mesh_id)
    for k in range(1, ndp):
        pl.semaphore_signal(barrier, inc=1, device_id={"seq": me, "dp": (d + k) % ndp},
                            device_id_type=mesh_id)

    def push(src, dst, send, recv, target, t_dp):
        return pltpu.make_async_remote_copy(
            src_ref=src, dst_ref=dst, send_sem=send, recv_sem=recv,
            device_id={"seq": target, "dp": t_dp}, device_id_type=mesh_id)

    def push_a(i):
        return push(box_a.at[i], home_a.at[me], a_send.at[i], a_recv.at[me], i, d)

    def push_g(i):
        return push(box_g.at[i], home_g.at[me], g_send.at[i], g_recv.at[me], i, d)

    def push_s(i):
        return push(seq_tile.at[me], seq_tile.at[me], s_send.at[i], s_recv.at[me], i, d)

    def push_d(j):
        return push(dp_tile.at[d], dp_tile.at[d], d_send.at[j], d_recv.at[d], me, j)

    def arrived(ref, sem):
        pltpu.make_async_copy(ref, ref, sem).wait()

    def prepare(i, carry):
        q = qc_ref[i, :, :span].astype(F32)
        c = qc_ref[i, :, span:].astype(F32)
        rows = [jnp.sum((q * q)[h * DH:(h + 1) * DH], axis=0, keepdims=True) for h in range(heads)]
        rows += [jnp.sum((q * c)[h * DH:(h + 1) * DH], axis=0, keepdims=True) for h in range(heads)]
        if 2 * heads < 8:
            rows.append(jnp.zeros((8 - 2 * heads, span), F32))
        cols[i] = jnp.transpose(jnp.concatenate(rows, axis=0))
        return carry

    lax.fori_loop(0, blocks, prepare, 0)
    sharp_at = dp_tile.at[d]
    sharp_at[...] = jnp.zeros((8, span), F32)
    key_at = lax.broadcasted_iota(jnp.int32, (span, span), 0)
    query_at = lax.broadcasted_iota(jnp.int32, (span, span), 1)
    tail = (lax.broadcasted_iota(jnp.int32, (16, 2 * span), 1) < span).astype(F32).astype(BF16)
    pl.semaphore_wait(barrier, blocks + ndp - 2)

    def block(k, carry):
        i = (me + blocks // 2 + k) % blocks
        other = pat_ref[i, 1]
        allowed = jnp.concatenate(
            [(i * span + key_at < length) | (key_at == query_at), other * span + key_at < length],
            axis=0)
        for h in range(heads):
            hs = slice(h * DH, (h + 1) * DH)
            qc = qc_ref[i, hs, :]
            qc_other = qc_ref[other, hs, :]
            q = qc[:, :span]
            c = qc[:, span:]
            keys = jnp.concatenate([q, qc_other[:, :span]], axis=1)
            key_cots = jnp.concatenate([c, qc_other[:, span:]], axis=1)
            both = dot(keys, qc, 0, 0)
            inner = both[:, :span]
            prob_grad = both[:, span:]
            cross = dot(key_cots, q, 0, 0)
            qf = q.astype(F32)
            cf = c.astype(F32)
            norm_row = jnp.sum(qf * qf, axis=0, keepdims=True)
            pair_row = jnp.sum(qf * cf, axis=0, keepdims=True)
            norm_col = jnp.concatenate([cols[i, :, h:h + 1], cols[other, :, h:h + 1]], axis=0)
            pair_col = jnp.concatenate(
                [cols[i, :, heads + h:heads + h + 1], cols[other, :, heads + h:heads + h + 1]], axis=0)
            factor = sharp_ref[h] * (1.0 / math.sqrt(DH))
            distance = norm_row + norm_col - 2.0 * inner
            weights = jnp.where(allowed, jnp.exp(-factor * distance), 0.0)
            total = jnp.sum(weights, axis=0, keepdims=True)
            soft = weights * (1.0 / total)
            low = soft.astype(BF16)
            row_inner = jnp.sum(soft * prob_grad, axis=0, keepdims=True)
            score = soft * (prob_grad - row_inner)
            dp_tile[d, h:h + 1, :] += jnp.sum(score * distance, axis=0, keepdims=True)
            coef = (-2.0 * factor * score).astype(BF16)
            row_total = jnp.sum(coef.astype(F32), axis=0, keepdims=True)
            gap = pair_row + pair_col - cross - prob_grad
            gap_mean = jnp.sum(soft * gap, axis=0, keepdims=True)
            adj = (-2.0 * factor * (soft * (gap - gap_mean))).astype(BF16)
            mixed = jnp.concatenate([coef, low], axis=1)
            left = dot(keys, mixed, 1, 0)
            box_a[i, 0, hs, :] = left[:, span:].astype(BF16)
            adjoint = dot(jnp.concatenate([keys, key_cots], axis=1),
                          jnp.concatenate([adj, low], axis=0), 1, 0)
            box_a[i, 1, hs, :] = adjoint.astype(BF16)
            lhs = jnp.concatenate([jnp.concatenate([-q, c], axis=1), tail], axis=0)
            right = dot(lhs, mixed, 1, 1)
            key_part = keys.astype(F32) * right[DH:DH + 1, :] + right[:DH]
            own[i, hs, :] = qf * row_total - left[:, :span] + key_part[:, :span]
            other_part[i, hs, :] = key_part[:, span:]
        pl.when(i != me)(lambda: push_a(i).start())
        return carry

    lax.fori_loop(0, blocks, block, 0)

    def finish(k, term):
        m = (me + blocks // 2 + k) % blocks

        def gather(i, total):
            chosen = jnp.where(pat_ref[i, 1] == m, 1.0, 0.0)
            return total + other_part[i] * chosen

        if blocks <= 8:
            g = own[m]
            for i in range(blocks):
                g = gather(i, g)
        else:
            g = lax.fori_loop(0, blocks, gather, own[m])
        box_g[m] = g.astype(BF16)
        pl.when(m != me)(lambda: push_g(m).start())
        return term + jnp.sum(g * qc_ref[m, :, span:].astype(F32), axis=0, keepdims=True)

    term_one = lax.fori_loop(0, blocks, finish, jnp.zeros((1, span), F32))
    for k in range(1, ndp):
        push_d((d + k) % ndp).start()
    home_a[me] = box_a[me]
    home_g[me] = box_g[me]
    fetch.wait()

    def take_a(k, carry):
        s = (me + k) % blocks
        pl.when(k > 0)(lambda: arrived(home_a.at[s], a_recv.at[s]))
        left_rows[s, :2 * span, :] = jnp.concatenate(
            [jnp.transpose(home_a[s, 0]), jnp.transpose(home_a[s, 1])], axis=0)
        return carry

    def split(v):
        high = v.astype(BF16).astype(F32)
        mid = (v - high).astype(BF16).astype(F32)
        rows = [high, mid, v - high - mid, jnp.zeros((13, v.shape[1]), F32)]
        return jnp.concatenate(rows, axis=0).astype(BF16)

    start_rows = split(start_ref[...])

    def power(s, total):
        column = jnp.sum(dot(start_rows, w_all[s], 1, 0), axis=0, keepdims=True)
        left_rows[s, 2 * span:, :] = split(column)
        return total + column * column

    column_sq = lax.fori_loop(0, blocks, power, jnp.zeros((1, width), F32))
    lax.fori_loop(0, blocks, take_a, 0)
    step = 256

    def product(rows_ref, r):
        at = pl.ds(pl.multiple_of(r * step, step), step)
        total = jnp.zeros((rows_ref.shape[1], step), F32)
        for s in range(blocks):
            total = total + dot(rows_ref[s], w_all[s, at, :], 1, 1)
        return at, total

    def outward(r, carry):
        at, total = product(left_rows, r)
        branch_ref[:, at] = total[:span].astype(BF16)
        adjoint_out[:, at] = total[span:2 * span]
        image[:, at] = jnp.sum(total[2 * span:], axis=0, keepdims=True)
        return carry

    lax.fori_loop(0, depth // step, outward, 0)

    def take_g(k, carry):
        s = (me + k) % blocks
        pl.when(k > 0)(lambda: arrived(home_g.at[s], g_recv.at[s]))
        grad_rows[s] = jnp.transpose(home_g[s])
        return carry

    lax.fori_loop(0, blocks, take_g, 0)

    def backward(r, term):
        at, total = product(grad_rows, r)
        low = total.astype(BF16)
        vjp_ref[:, at] = low
        part = low.astype(F32) * adjoint_out[:, at]
        for n in range(step // span):
            term = term + jnp.sum(part[:, n * span:(n + 1) * span], axis=0, keepdims=True)
        return term

    image_sq = jnp.sum(image[...] * image[...], axis=1, keepdims=True)
    spec_ref[...] = image[...] / jnp.sqrt(image_sq / depth + 1e-06)
    norm = jnp.sqrt(image_sq / (jnp.sum(column_sq, axis=1, keepdims=True) + 1e-06))
    stat_ref[16:] = jnp.broadcast_to(norm, (8, span))
    term_two = lax.fori_loop(0, depth // step, backward, jnp.zeros((1, span), F32))
    seq_tile[me] = jnp.concatenate([term_one, term_two, jnp.zeros((6, span), F32)], axis=0)
    for k in range(1, blocks):
        push_s((me + k) % blocks).start()
    for k in range(1, ndp):
        j = (d + k) % ndp
        arrived(dp_tile.at[j], d_recv.at[j])
        push_d(j).wait_send()
    for k in range(1, blocks):
        i = (me + k) % blocks
        push_a(i).wait_send()
        push_g(i).wait_send()
        arrived(seq_tile.at[i], s_recv.at[i])
        push_s(i).wait_send()
    stat_ref[:8] = jnp.broadcast_to(
        jnp.sum(jnp.sum(seq_tile[...], axis=0), axis=1, keepdims=True), (8, span))
    stat_ref[8:16] = jnp.broadcast_to(
        jnp.sum(jnp.sum(dp_tile[...], axis=0), axis=1, keepdims=True), (8, span))


def attention(ndp, qc, w_all, sharpness, pattern, lengths, start_vector):
    blocks, width, pair = qc.shape
    span = pair // 2
    depth = w_all.shape[1]
    heads = sharpness.shape[0]
    smem = pl.BlockSpec(memory_space=pltpu.SMEM)
    vmem = pl.BlockSpec(memory_space=pltpu.VMEM)
    sem = pltpu.SemaphoreType.DMA
    return pl.pallas_call(
        functools.partial(attention_kernel, heads, ndp),
        out_shape=(jax.ShapeDtypeStruct((span, depth), BF16),
                   jax.ShapeDtypeStruct((span, depth), BF16),
                   jax.ShapeDtypeStruct((24, span), F32),
                   jax.ShapeDtypeStruct((1, depth), F32)),
        in_specs=[vmem, pl.BlockSpec(memory_space=pl.ANY), smem, smem, smem, vmem],
        out_specs=(vmem, vmem, vmem, vmem),
        scratch_shapes=[pltpu.VMEM((1, depth), F32),
                        pltpu.VMEM((blocks, span, max(8, 2 * heads)), F32),
                        pltpu.VMEM((blocks, width, span), F32),
                        pltpu.VMEM((blocks, width, span), F32),
                        pltpu.VMEM((blocks, 2, width, span), BF16),
                        pltpu.VMEM((blocks, width, span), BF16),
                        pltpu.VMEM((blocks, 2, width, span), BF16),
                        pltpu.VMEM((blocks, width, span), BF16),
                        pltpu.VMEM((blocks, 2 * span + 16, width), BF16),
                        pltpu.VMEM((blocks, span, width), BF16),
                        pltpu.VMEM((span, depth), F32),
                        pltpu.VMEM((blocks, depth, width), BF16),
                        pltpu.VMEM((blocks, 8, span), F32),
                        pltpu.VMEM((ndp, 8, span), F32),
                        sem, sem((blocks,)), sem((blocks,)), sem((blocks,)), sem((blocks,)),
                        sem((blocks,)), sem((blocks,)), sem((ndp,)), sem((ndp,))],
        compiler_params=pltpu.CompilerParams(collective_id=1, has_side_effects=True,
                                             vmem_limit_bytes=56 * 1024 * 1024),
        name="attention",
    )(qc, w_all, sharpness, pattern, lengths, start_vector.reshape(1, depth))


def keep_kernel(a_ref, b_ref, a_out, b_out):
    a_out[...] = a_ref[...]
    b_out[...] = b_ref[...]


def keep(a, b):
    vmem = pl.BlockSpec(memory_space=pltpu.VMEM)
    shape = jax.ShapeDtypeStruct(a.shape, a.dtype)
    return pl.pallas_call(keep_kernel, out_shape=(shape, shape), in_specs=[vmem, vmem],
                          out_specs=(vmem, vmem), name="keep")(a, b)


def gather_kernel(ndp, groups, x_ref, p_ref, w_ref, len_ref, w_out, got, both, outbox, recv, send, a2a_recv, a2a_send):
    span, depth = x_ref.shape
    width = w_ref.shape[1]
    lines, rows = groups // 2, depth // ndp
    ys = ndp // 2
    me, d = lax.axis_index("seq"), lax.axis_index("dp")
    z, x = me // 2, me % 2
    y, core = d // 2, d % 2

    def seq_id(s):
        return {"seq": s, "dp": d}

    def dp_id(t):
        return {"seq": me, "dp": t}

    barrier = pltpu.get_barrier_semaphore()
    for k in range(1, groups):
        pl.semaphore_signal(barrier, inc=1, device_id=seq_id((me + k) % groups),
                            device_id_type=pl.DeviceIdType.MESH)
    pl.semaphore_signal(barrier, inc=1, device_id=dp_id(d + 1 - 2 * core),
                        device_id_type=pl.DeviceIdType.MESH)
    for k in range(1, ys):
        pl.semaphore_signal(barrier, inc=1, device_id=dp_id(((y + k) % ys) * 2 + core),
                            device_id_type=pl.DeviceIdType.MESH)
    pl.semaphore_wait(barrier, groups + ys - 1)

    def piece(s, owner, kind, target, own=False):
        at = pl.ds(pl.multiple_of(owner * rows, rows), rows)
        src = w_ref.at[at] if own else w_out.at[s, at]
        return pltpu.make_async_remote_copy(
            src_ref=src, dst_ref=w_out.at[s, at], send_sem=send.at[kind, s],
            recv_sem=recv.at[owner, s], device_id=target, device_id_type=pl.DeviceIdType.MESH)

    def landed(s, owner):
        at = pl.ds(pl.multiple_of(owner * rows, rows), rows)
        pltpu.make_async_copy(w_out.at[s, at], w_out.at[s, at], recv.at[owner, s]).wait()

    up, down, across = seq_id((me + 2) % groups), seq_id((me + groups - 2) % groups), seq_id(me + 1 - 2 * x)
    mate = dp_id(d + 1 - 2 * core)

    def order(t):
        p, side = t // 2, t % 2
        m = jnp.minimum(z, lines - 1 - z)
        near = jnp.where(p % 2 == 1, z + (p + 1) // 2, z - p // 2)
        far = jnp.where(2 * z < lines, p, lines - 1 - p)
        zs = jnp.where(p <= 2 * m, near, far)
        xs = (x + side) % 2
        return zs * 2 + xs, zs, xs

    pl.when(z + 1 < lines)(lambda: piece(me, d, 0, up, True).start())
    pl.when(z > 0)(lambda: piece(me, d, 1, down, True).start())
    piece(me, d, 2, across, True).start()
    for k in range(1, ys):
        piece(me, ((y + k) % ys) * 2 + core, 3 + k, across, True).start()
    w_out[me] = w_ref[...]
    both[:span] = x_ref[...]
    valid = me * span + lax.broadcasted_iota(jnp.int32, (span, 1), 0) < len_ref[0]
    both[span:] = jnp.where(valid, p_ref[...].astype(F32), 0.0).astype(BF16)

    def stage_a(t):
        s, zs, xs = order(t)
        landed(s, d)

        @pl.when(xs == x)
        def _():
            pl.when((zs < z) & (z + 1 < lines))(lambda: piece(s, d, 0, up).start())
            pl.when((zs > z) & (z > 0))(lambda: piece(s, d, 1, down).start())
            piece(s, d, 2, across).start()

        @pl.when(t > 1)
        def _():
            for k in range(1, ys):
                piece(s, d, 3 + k, dp_id(((y + k) % ys) * 2 + core)).start()

        piece(s, d, 3, mate).start()

    def stage_b(t):
        s, zs, xs = order(t)
        for k in range(1, ys):
            owner = ((y + k) % ys) * 2 + core
            landed(s, owner)
            piece(s, owner, 2 + ys + k, mate).start()

    def out_copy(s):
        return pltpu.make_async_remote_copy(
            src_ref=outbox.at[s], dst_ref=got.at[me], send_sem=a2a_send.at[s],
            recv_sem=a2a_recv.at[me], device_id=seq_id(s), device_id_type=pl.DeviceIdType.MESH)

    def stage_c(t):
        s, zs, xs = order(t)

        @pl.when(t > 0)
        def _():
            for k in range(ys):
                landed(s, ((y + k) % ys) * 2 + 1 - core)

        w = w_out[s]
        res = jnp.transpose(dot(both[...], w, 1, 0)).astype(BF16)

        @pl.when(t > 0)
        def _():
            outbox[s] = res
            out_copy(s).start()

        @pl.when(t == 0)
        def _():
            got[me] = res

    lag_b, lag_c = 4, 5

    def tick(t, carry):
        pl.when((t > 0) & (t < groups))(lambda: stage_a(t))
        pl.when((t - lag_b > 0) & (t - lag_b < groups))(lambda: stage_b(t - lag_b))
        pl.when(t - lag_c >= 0)(lambda: stage_c(t - lag_c))
        return carry

    lax.fori_loop(0, groups + lag_c, tick, 0)

    def drain(t, carry):
        s, zs, xs = order(t)
        pl.when((xs == x) & (zs <= z) & (z + 1 < lines))(lambda: piece(s, d, 0, up).wait_send())
        pl.when((xs == x) & (zs >= z) & (z > 0))(lambda: piece(s, d, 1, down).wait_send())
        pl.when(xs == x)(lambda: piece(s, d, 2, across).wait_send())

        @pl.when(t != 1)
        def _():
            for k in range(1, ys):
                piece(s, d, 3 + k, mate).wait_send()

        @pl.when(t > 0)
        def _():
            for k in range(1, ys):
                piece(s, d, 2 + ys + k, mate).wait_send()
            piece(s, d, 3, mate).wait_send()
            out_copy(s).wait_send()
            pltpu.make_async_copy(got.at[s], got.at[s], a2a_recv.at[s]).wait()

        return carry

    lax.fori_loop(0, groups, drain, 0)


def gather_project(ndp, groups, tokens, probe_rows, w_query, lengths):
    span, depth = tokens.shape
    width = w_query.shape[1]
    smem = pl.BlockSpec(memory_space=pltpu.SMEM)
    vmem = pl.BlockSpec(memory_space=pltpu.VMEM)
    return pl.pallas_call(
        functools.partial(gather_kernel, ndp, groups),
        out_shape=(jax.ShapeDtypeStruct((groups, depth, width), BF16),
                   jax.ShapeDtypeStruct((groups, width, 2 * span), BF16)),
        in_specs=[vmem, vmem, vmem, smem],
        out_specs=(vmem, vmem),
        scratch_shapes=[pltpu.VMEM((2 * span, depth), BF16),
                        pltpu.VMEM((groups, width, 2 * span), BF16),
                        pltpu.SemaphoreType.DMA((ndp, groups)),
                        pltpu.SemaphoreType.DMA((2 + ndp, groups)),
                        pltpu.SemaphoreType.DMA((groups,)),
                        pltpu.SemaphoreType.DMA((groups,))],
        compiler_params=pltpu.CompilerParams(collective_id=0, has_side_effects=True,
                                             vmem_limit_bytes=56 * 1024 * 1024),
        name="gather_project",
    )(tokens, probe_rows, w_query, lengths)


def shards(inputs, w_query, sharpness, pattern, lengths, probes, start_vector):
    tokens = inputs[0]
    probe_rows = probes[0]
    length = lengths[0]
    rows_here = tokens.shape[0]
    groups = lax.axis_size("seq")
    inner_here = w_query.shape[1]
    inner = inner_here * groups
    w_all, got = gather_project(
        lax.axis_size("dp"), groups, tokens, probe_rows, w_query, lengths)
    branch, probe_vjp, stats, spec = attention(
        lax.axis_size("dp"), got, w_all, sharpness, pattern, lengths, start_vector)
    branch, probe_vjp = keep(branch, probe_vjp)
    heads = sharpness.shape[0]
    seq_total = groups * rows_here
    term_total = stats[:2, 0] / (length.astype(F32) * inner)
    scale_down = 1.0 / (lax.axis_size("dp") * seq_total * DH)
    sharp_grad = stats[8:8 + heads, 0] * (-1.0 / math.sqrt(DH)) * scale_down
    spec_vector = spec.reshape(-1)
    spec_norm = stats[16, :1]
    return (branch[None], probe_vjp[None], term_total.reshape(1, 2), sharp_grad, spec_vector, spec_norm)


def solution(mesh):
    placed = (
        P("dp", "seq", None),
        P(None, "seq"),
        P("seq"),
        P(),
        P("dp"),
        P("dp", "seq", None),
        P(),
    )
    return jax.shard_map(
        shards,
        mesh=mesh,
        in_specs=placed,
        out_specs=(P("dp", "seq", None), P("dp", "seq", None), P("dp", None), P("seq"), P(), P()),
        check_vma=False,
    )
```
